32 devices in a mesh: gx: 4 (over z), gy: 4 (over y, x), gz: 2 (over core).
Axes of the slice: x: 2, y: 2, z: 4, core: 2. Of those that a mesh axis runs over, the one named last changes fastest.
Arguments:
- species_field: float32 [8, 384, 6144], P('gz', 'gx', 'gy'), may hold values from -24 to 24
- start_first: float32 [384, 96], replicated, may hold values from -0.3125 to 0.3125
- start_second: float32 [384, 96], replicated, may hold values from -0.3125 to 0.3125
Outputs:
- factor_first: float32 [384, 96], replicated
- factor_second: float32 [384, 96], replicated
- core_tensor: float32 [16, 8, 96, 96], P('gx', 'gz', 'gy')
The draws below stay inside these ranges and needn't reach their ends.
All inputs are finite; a program needn't handle non-finite values.
Results may differ from the reference program's by a relative error of at most 0.0003.
Values sent between devices are 32-bit elements; how exact they have to be, the bound alone decides.
A program may use at most 64 MiB of HBM per device.

```python
import math
import jax
import jax.numpy as jnp
from jax import lax

S = 16
NX = 384
NY = 384
RANK = 96
ITERS = 2
NZ = 8


def scaled_range(subkey, length_of, lowest, highest):
    return jnp.exp(jax.random.uniform(subkey, (length_of,), jnp.float32, math.log(lowest), math.log(highest)))


def draw_species_field(key, part):
    subkeys = jax.random.split(key, 9)
    signal_rank = max(RANK // 2, 1)
    left_factor = jax.random.truncated_normal(subkeys[0], -4.0, 4.0, (NX, signal_rank), jnp.float32)
    left_factor = left_factor * scaled_range(subkeys[1], signal_rank, 0.5, 2.0)[None, :] / math.sqrt(signal_rank)
    right_factor = jax.random.truncated_normal(subkeys[2], -4.0, 4.0, (NY, signal_rank), jnp.float32)
    right_factor = right_factor * scaled_range(subkeys[3], signal_rank, 0.5, 2.0)[None, :] / math.sqrt(signal_rank)
    inner_core = jax.random.truncated_normal(subkeys[4], -4.0, 4.0, (NZ, signal_rank, signal_rank, S), jnp.float32)
    region = jax.random.uniform(subkeys[5], (NZ, S), jnp.float32, 0.4, 1.6)
    inner_core = inner_core * region[:, None, None, :]
    mixed = jnp.einsum('zabs,ia->zibs', inner_core, left_factor)
    signal = jnp.einsum('zibs,jb->zijs', mixed, right_factor)
    row_scale = scaled_range(subkeys[6], NX, 0.5, 1.5)
    column_scale = scaled_range(subkeys[7], NY, 0.5, 1.5)
    noise_part = jax.random.truncated_normal(subkeys[8], -4.0, 4.0, (NZ, NX, NY, S), jnp.float32)
    noise_part = noise_part * (row_scale[:, None] * column_scale[None, :])[None, :, :, None]
    whole = jnp.clip(signal + noise_part, -24.0, 24.0)
    return whole.reshape(NZ, NX, NY * S).astype(jnp.float32)


def centred(stream_key, extent, deviation, bound, dtype=jnp.bfloat16):
    return jnp.clip(deviation * jax.random.normal(stream_key, extent, jnp.float32), -bound, bound).astype(dtype)


def setup_inputs(seed: int = 0) -> dict:
    key_list = jax.random.split(jax.random.key(seed), 4)
    return {
        "species_field": draw_species_field(jax.random.fold_in(key_list[3], 71), 0),
        "start_first": centred(key_list[1], (NX, RANK), NX ** -0.5, 0.3125, jnp.float32),
        "start_second": centred(key_list[2], (NY, RANK), NY ** -0.5, 0.3125, jnp.float32),
    }


exact_precision = lax.Precision.HIGHEST

def power_steps(gram, start):
    current = start
    for turn in range(ITERS):
        images = jnp.dot(gram, current, precision=exact_precision)
        cross_gram = jnp.dot(images.T, images, precision=exact_precision)
        lower_factor = jnp.linalg.cholesky(cross_gram)
        current = lax.linalg.triangular_solve(lower_factor, images, left_side=False, lower=True, transpose_a=True)
    return current

def reference(species_field, start_first, start_second):
    field = species_field.reshape(NZ, NX, NY, S)
    gram_first = jnp.einsum('zics,zjcs->ij', field, field, precision=exact_precision)
    factor_first = power_steps(gram_first, start_first)
    projected = jnp.einsum('zics,ir->zrcs', field, factor_first, precision=exact_precision)
    gram_second = jnp.einsum('zrjs,zrks->jk', projected, projected, precision=exact_precision)
    factor_second = power_steps(gram_second, start_second)
    core_tensor = jnp.einsum('zrjs,jq->szrq', projected, factor_second, precision=exact_precision)
    return (factor_first, factor_second, core_tensor)
```

```python
import functools

import jax
import jax.numpy as jnp
from jax import lax
from jax.experimental import pallas as pl
from jax.experimental.pallas import tpu as pltpu
from jax.sharding import PartitionSpec as P

S = 16
ITERS = 2
PANEL = 24
LANES = 128
GRANT = 32 * 2**20
MESH = pl.DeviceIdType.MESH
VMEM = pl.BlockSpec(memory_space=pltpu.VMEM)

exact_precision = lax.Precision.HIGHEST


def dot_dims(a, b, contract_a, contract_b):
    return lax.dot_general(
        a, b, (((contract_a,), (contract_b,)), ((), ())),
        precision=exact_precision, preferred_element_type=jnp.float32,
    )


def partners(n, me):
    if n == 4:
        return [3 - me, lax.rem(me + 2, 4), me + 1 - 2 * lax.rem(me, 2)]
    return [lax.rem(me + d, n) for d in range(1, n)]


def send(src, dst, send_sem, recv_sem, target):
    copy = pltpu.make_async_remote_copy(
        src_ref=src, dst_ref=dst, send_sem=send_sem, recv_sem=recv_sem,
        device_id=target, device_id_type=MESH,
    )
    copy.start()
    return copy


def say_hello(targets):
    barrier = pltpu.get_barrier_semaphore()
    for target in targets:
        pl.semaphore_signal(barrier, inc=1, device_id=target, device_id_type=MESH)


def hear_hello(targets):
    pl.semaphore_wait(pltpu.get_barrier_semaphore(), len(targets))


def greet(targets):
    say_hello(targets)
    hear_hello(targets)


def axis_peers(axes, sizes):
    return [{axis: p} for axis, n in zip(axes, sizes) for p in partners(n, lax.axis_index(axis))]


def reduce_blocks(axes, sizes, splits, x_ref, o_ref, scratch):
    levels = len(axes)
    landing, totals = scratch[:levels], scratch[levels : 2 * levels - 1]
    send_sems, recv_sems = scratch[2 * levels - 1 :]
    me = [lax.axis_index(axis) for axis in axes]
    peers = [partners(n, m) for n, m in zip(sizes, me)]
    spot = [m if split > 1 else 0 for m, split in zip(me, splits)]
    sem = 0
    held = x_ref
    for level in range(levels):
        axis, n, split = axes[level], sizes[level], splits[level]
        land = landing[level]
        copies = []
        for p in peers[level]:
            src = held.at[p] if split > 1 else held.at[0]
            copies.append(send(src, land.at[me[level]], send_sems.at[sem], recv_sems.at[sem], {axis: p}))
            sem += 1
        land[me[level]] = held[spot[level]]
        for copy in copies:
            copy.wait()
        total = land[0]
        for source in range(1, n):
            total = total + land[source]
        if level < levels - 1:
            totals[level][...] = total
            held = totals[level]
        else:
            o_ref[tuple(spot)] = total

    for level in reversed(range(levels)):
        if splits[level] == 1:
            continue
        block = o_ref.at[tuple(spot[: level + 1])]
        copies = []
        for p in peers[level]:
            copies.append(send(block, block, send_sems.at[sem], recv_sems.at[sem], {axes[level]: p}))
            sem += 1
        for copy in copies:
            copy.wait()


def all_reduce_kernel(axes, sizes, splits, x_ref, o_ref, *scratch):
    greet(axis_peers(axes, sizes))
    reduce_blocks(axes, sizes, splits, x_ref, o_ref, scratch)


def reduce_plan(rows, columns, sizes):
    splits = []
    for n in sizes:
        splits.append(n if rows % n == 0 else 1)
        rows //= splits[-1]
    scratch = [
        pltpu.VMEM((n, *splits[level + 1 :], rows, columns), jnp.float32)
        for level, n in enumerate(sizes)
    ]
    scratch += [pltpu.VMEM((*splits[level + 1 :], rows, columns), jnp.float32) for level in range(len(sizes) - 1)]
    count = sum(n - 1 for n in sizes) + sum(n - 1 for n, split in zip(sizes, splits) if split > 1)
    scratch += [pltpu.SemaphoreType.DMA((count,)), pltpu.SemaphoreType.DMA((count,))]
    return splits, (*splits, rows, columns), scratch


def all_reduce(x, axes, sizes, collective_id):
    splits, blocked, scratch = reduce_plan(*x.shape, sizes)
    out = pl.pallas_call(
        functools.partial(all_reduce_kernel, axes, sizes, splits),
        out_shape=jax.ShapeDtypeStruct(blocked, jnp.float32),
        in_specs=[VMEM],
        out_specs=VMEM,
        scratch_shapes=scratch,
        compiler_params=pltpu.CompilerParams(collective_id=collective_id, has_side_effects=True),
    )(x.reshape(blocked))
    return out.reshape(x.shape)


def fibres_kernel(n, x_ref, o_ref, send_sems, recv_sems):
    me = lax.axis_index("gx")
    depth, rows, width = x_ref.shape[0], x_ref.shape[1], o_ref.shape[-1]
    peers = partners(n, me)
    greet([{"gx": p} for p in peers])
    copies = []
    for turn, p in enumerate(peers):
        columns = pl.ds(pl.multiple_of(p * width, width), width)
        copies.append(
            send(x_ref.at[:, :, columns], o_ref.at[:, me], send_sems.at[turn], recv_sems.at[turn], {"gx": p})
        )
    own = pl.ds(pl.multiple_of(me * width, width), width)
    for level in range(depth):
        o_ref[level, me] = x_ref[level, :, own]
    for copy in copies:
        copy.wait()


def gather_fibres(field, n):
    depth, rows, columns = field.shape
    width = columns // n
    if width % 128:
        return lax.all_to_all(field, "gx", split_axis=2, concat_axis=1, tiled=True)
    out = pl.pallas_call(
        functools.partial(fibres_kernel, n),
        out_shape=jax.ShapeDtypeStruct((depth, n, rows, width), jnp.float32),
        in_specs=[VMEM],
        out_specs=VMEM,
        scratch_shapes=[pltpu.SemaphoreType.DMA((n - 1,)), pltpu.SemaphoreType.DMA((n - 1,))],
        compiler_params=pltpu.CompilerParams(collective_id=0, has_side_effects=True),
    )(field)
    return out.reshape(depth, n * rows, width)


def exchange_kernel(nx, ny, x_ref, o_ref, send_sems, recv_sems):
    mx, my = lax.axis_index("gx"), lax.axis_index("gy")
    peers = [(px, my) for px in partners(nx, mx)]
    for py in partners(ny, my):
        peers += [(px, py) for px in partners(nx, mx) + [mx]]
    greet([{"gx": px, "gy": py} for px, py in peers])
    copies = []
    for turn, (px, py) in enumerate(peers):
        copies.append(
            send(x_ref.at[py, px], o_ref.at[my, mx], send_sems.at[turn], recv_sems.at[turn], {"gx": px, "gy": py})
        )
    o_ref[my, mx] = x_ref[my, mx]
    for copy in copies:
        copy.wait()


def exchange(blocks):
    ny, nx = blocks.shape[:2]
    count = nx * ny - 1
    return pl.pallas_call(
        functools.partial(exchange_kernel, nx, ny),
        out_shape=jax.ShapeDtypeStruct(blocks.shape, jnp.float32),
        in_specs=[VMEM],
        out_specs=VMEM,
        scratch_shapes=[pltpu.SemaphoreType.DMA((count,)), pltpu.SemaphoreType.DMA((count,))],
        compiler_params=pltpu.CompilerParams(collective_id=1, has_side_effects=True),
    )(blocks)


def inverse_lower(cross):
    rank = cross.shape[0]
    panel = PANEL if rank % PANEL == 0 else 8
    row = lax.broadcasted_iota(jnp.int32, (rank, rank), 0)
    column = lax.broadcasted_iota(jnp.int32, (rank, rank), 1)
    rest = cross
    rest_inverse = jnp.where(row == column, 1.0, 0.0).astype(jnp.float32)
    local_row = lax.broadcasted_iota(jnp.int32, (panel, rank), 0)
    done = []
    for start in range(0, rank, panel):
        upper = rest[:panel]
        inverse = rest_inverse[:panel]
        columns = [
            jnp.broadcast_to(upper[:, start + j : start + j + 1], (panel, rank)) for j in range(panel)
        ]
        diagonal = jnp.ones((panel, rank), jnp.float32)
        for j in range(panel):
            pivot = jnp.broadcast_to(columns[j][j : j + 1], (panel, rank))
            diagonal = jnp.where(local_row == j, pivot, diagonal)
            if j == panel - 1:
                break
            factor = jnp.where(local_row > j, columns[j] * (1.0 / pivot), 0.0)
            for other in range(j + 1, panel):
                columns[other] = columns[other] - factor * columns[other][j : j + 1]
            upper = upper - factor * upper[j : j + 1]
            inverse = inverse - factor * inverse[j : j + 1]
        done.append(inverse * (1.0 / jnp.sqrt(diagonal)))
        if start + panel < rank:
            scaled = upper / diagonal
            update = dot_dims(scaled, jnp.concatenate([upper, inverse], axis=1), 0, 0)
            after = start + panel
            rest = rest[panel:] - update[after:, :rank]
            rest_inverse = rest_inverse[panel:] - update[after:, rank:]
    return jnp.concatenate(done, axis=0)


def power_general_kernel(gram_ref, start_ref, out_ref):
    current = start_ref[...]
    for turn in range(ITERS):
        images = dot_dims(gram_ref[...], current, 1, 0)
        cross = dot_dims(images, images, 0, 0)
        current = dot_dims(images, inverse_lower(cross), 1, 1)
    out_ref[...] = current


def leading(gram, start):
    return pl.pallas_call(
        power_general_kernel,
        out_shape=jax.ShapeDtypeStruct(start.shape, jnp.float32),
        in_specs=[VMEM, VMEM],
        out_specs=VMEM,
    )(gram, start)


def local_general(nx, ny, nz, species_field, start_first, start_second):
    axes, sizes = ("gz", "gy", "gx"), (nz, ny, nx)
    fibres = gather_fibres(species_field, nx)
    partial_gram = jnp.einsum("zic,zjc->ij", fibres, fibres, precision=exact_precision)
    gram_first = all_reduce(partial_gram, axes, sizes, 2)
    factor_first = leading(gram_first, start_first)

    depth = fibres.shape[0]
    cells = fibres.shape[2] // S
    rank = start_first.shape[1]
    species, ranks = S // nx, rank // ny
    projected = jnp.einsum("zim,ir->zmr", fibres, factor_first, precision=exact_precision)
    blocks = projected.reshape(depth, cells, nx, species, ny, ranks)
    blocks = blocks.transpose(4, 2, 1, 3, 0, 5).reshape(ny, nx, cells, species * depth * ranks)
    columns = exchange(blocks)
    columns = columns.reshape(ny * nx * cells, species * depth * ranks)
    partial_second = dot_dims(columns, columns, 1, 1)
    gram_second = all_reduce(partial_second, axes, sizes, 3)
    factor_second = leading(gram_second, start_second)
    core = dot_dims(columns, factor_second, 0, 0)
    core = core.reshape(species, depth, ranks, factor_second.shape[1])
    return (factor_first, factor_second, core)


def upper_blocks(count):
    return [(a, b) for a in range(count) for b in range(a, count)]


def add_gram(gram_ref, parts, contract, first):
    for slot, (a, b) in enumerate(upper_blocks(len(parts))):
        block = pl.ds(slot * LANES, LANES)
        term = dot_dims(parts[a], parts[b], contract, contract)
        gram_ref[block, :] = term if first else gram_ref[block, :] + term


def times_gram(current, gram_ref):
    count = current.shape[1] // LANES
    sums = [None] * count
    for slot, (a, b) in enumerate(upper_blocks(count)):
        block = gram_ref[slot * LANES : (slot + 1) * LANES, :]
        terms = [(b, a, 0)] if a == b else [(b, a, 0), (a, b, 1)]
        for to, of, contract in terms:
            term = dot_dims(current[:, of * LANES : (of + 1) * LANES], block, 1, contract)
            sums[to] = term if sums[to] is None else sums[to] + term
    return jnp.concatenate(sums, axis=1)


def power_steps(gram_ref, current):
    for turn in range(ITERS):
        images = times_gram(current, gram_ref)
        cross = dot_dims(images, images, 1, 1)
        current = dot_dims(inverse_lower(cross), images, 1, 0)
    return current


def second_power_kernel(gram_ref, start_ref, rows_ref, first_ref, first_out_ref, out_ref, core_ref):
    first_out_ref[...] = first_ref[...]
    current = power_steps(gram_ref, start_ref[...])
    out_ref[...] = current
    core_ref[...] = dot_dims(rows_ref[...], current, 1, 1)


def species_major(block, order):
    high = block.astype(jnp.bfloat16)
    left = block - high.astype(jnp.float32)
    middle = left.astype(jnp.bfloat16)
    low = (left - middle.astype(jnp.float32)).astype(jnp.bfloat16)
    moved = [
        lax.dot_general(part, order, (((1,), (0,)), ((), ())), preferred_element_type=jnp.float32)
        for part in (high, middle, low)
    ]
    return (moved[0] + moved[1]) + moved[2]


def first_exchange(n, targets, x_ref, start_load, field, fibres, gram, packed, load_sems, send_sems, recv_sems):
    me = lax.axis_index("gx")
    depth, rows, columns = field.shape
    span = n * LANES
    cells = span // S
    width = columns // n
    loads = [pltpu.make_async_copy(x_ref.at[z], field.at[z], load_sems.at[z]) for z in range(depth)]
    for load in loads + [start_load]:
        load.start()
    say_hello(targets)
    peers = partners(n, me)
    source = lax.broadcasted_iota(jnp.int32, (span, span), 0)
    target = lax.broadcasted_iota(jnp.int32, (span, span), 1)
    species = lax.shift_right_logical(target, cells.bit_length() - 1)
    order = jnp.where(source == (target & (cells - 1)) * S + species, 1.0, 0.0).astype(jnp.bfloat16)
    copies = []
    for level in range(depth):
        loads[level].wait()
        for chunk in range(columns // span):
            moved = species_major(field[level, :, chunk * span : (chunk + 1) * span], order)
            lanes = pl.ds(chunk * LANES, LANES)
            for p in range(n):
                packed[level, p, :, lanes] = moved[:, p * LANES : (p + 1) * LANES]
        if level == 0:
            hear_hello(targets)
        turns = list(enumerate(peers))
        if level > 0:
            turns = turns[-1:] + turns[:-1]
        for turn, p in turns:
            sem = level * (n - 1) + turn
            copies.append(
                send(packed.at[level, p], fibres.at[level, me], send_sems.at[sem], recv_sems.at[sem], {"gx": p})
            )
        fibres[level, me] = packed[level, me]
    for level in range(depth):
        for copy in copies[level * (n - 1) : (level + 1) * (n - 1)]:
            copy.wait()
        whole = fibres[level].reshape(n * rows, width)
        parts = [whole[a : a + LANES] for a in range(0, n * rows, LANES)]
        add_gram(gram, parts, 1, level == 0)
    start_load.wait()


def second_exchange(n, cells, factor, fibres, rows_ref, gram, packed, land, send_sems, recv_sems):
    me = lax.axis_index("gy")
    depth, ranks, width = packed.shape[0], packed.shape[2], packed.shape[3]
    peers = partners(n, me)
    copies = []
    for level in range(depth):
        whole = fibres[level].reshape(factor.shape[1], width)
        packed[level] = dot_dims(factor, whole, 1, 0).reshape(n, ranks, width)
        for turn, p in enumerate(peers):
            sem = level * (n - 1) + turn
            copies.append(
                send(packed.at[level, p], land.at[me, level], send_sems.at[sem], recv_sems.at[sem], {"gy": p})
            )
        land[me, level] = packed[level, me]
    lane_group = lax.shift_right_logical(
        lax.broadcasted_iota(jnp.int32, (ranks, LANES), 1), cells.bit_length() - 1
    )
    for level in range(depth):
        for copy in copies[level * (n - 1) : (level + 1) * (n - 1)]:
            copy.wait()
        chunks = width // LANES
        for tile in range(chunks):
            for s in range(n):
                merged = None
                for g in range(n):
                    t, chunk = divmod(n * tile + g, chunks)
                    turned = land[t, level, :, chunk * LANES : (chunk + 1) * LANES]
                    if g != s:
                        turned = pltpu.roll(turned, cells * ((g - s) % n), 1)
                    merged = turned if g == 0 else jnp.where(lane_group == g, turned, merged)
                rows_ref[s, level, :, tile * LANES : (tile + 1) * LANES] = merged
        whole = rows_ref[:, level].reshape(n * ranks, width)
        parts = [whole[:, a : a + LANES] for a in range(0, width, LANES)]
        add_gram(gram, parts, 0, level == 0)


def stages_kernel(axes, sizes, cells, splits, x_ref, start_ref, factor_ref, rows_ref, gram_ref, *scratch):
    ny, nx = sizes[1], sizes[2]
    targets = axis_peers(axes, sizes)
    gram, field, fibres, packed, load_sems, send_first, recv_first = scratch[:7]
    packed_second, land, send_second, recv_second, start, start_sem = scratch[7:13]
    half = (len(scratch) - 13) // 2
    reduces = scratch[13 : 13 + half], scratch[13 + half :]
    start_load = pltpu.make_async_copy(start_ref, start, start_sem)

    def reduced(reduce_scratch, into):
        held, total = reduce_scratch[0], reduce_scratch[1]
        held[...] = gram[...].reshape(held.shape)
        reduce_blocks(axes, sizes, splits, held, total, reduce_scratch[2:])
        into[...] = total[...].reshape(into.shape)

    first_exchange(nx, targets, x_ref, start_load, field, fibres, gram, packed, load_sems, send_first, recv_first)
    reduced(reduces[0], gram)
    factor = power_steps(gram, start[...])
    factor_ref[...] = factor
    second_exchange(ny, cells, factor, fibres, rows_ref, gram, packed_second, land, send_second, recv_second)
    reduced(reduces[1], gram_ref)


def stages(field, start, axes, sizes, cells):
    ny, nx = sizes[1], sizes[2]
    depth, rows, columns = field.shape
    rank, extent = start.shape
    width = columns // nx
    ranks = rank // ny
    gram_shape = (len(upper_blocks(extent // LANES)) * LANES, LANES)
    splits, blocked, reduce_scratch = reduce_plan(*gram_shape, sizes)
    reduce_scratch = [pltpu.VMEM(blocked, jnp.float32)] * 2 + reduce_scratch
    first, second = depth * (nx - 1), depth * (ny - 1)
    return pl.pallas_call(
        functools.partial(stages_kernel, axes, sizes, cells, splits),
        out_shape=(
            jax.ShapeDtypeStruct((rank, extent), jnp.float32),
            jax.ShapeDtypeStruct((ny, depth, ranks, width), jnp.float32),
            jax.ShapeDtypeStruct(gram_shape, jnp.float32),
        ),
        in_specs=[pl.BlockSpec(memory_space=pltpu.HBM)] * 2,
        out_specs=(VMEM, VMEM, VMEM),
        scratch_shapes=[
            pltpu.VMEM(gram_shape, jnp.float32),
            pltpu.VMEM((depth, rows, columns), jnp.float32),
            pltpu.VMEM((depth, nx, rows, width), jnp.float32),
            pltpu.VMEM((depth, nx, rows, width), jnp.float32),
            pltpu.SemaphoreType.DMA((depth,)),
            pltpu.SemaphoreType.DMA((first,)),
            pltpu.SemaphoreType.DMA((first,)),
            pltpu.VMEM((depth, ny, ranks, width), jnp.float32),
            pltpu.VMEM((ny, depth, ranks, width), jnp.float32),
            pltpu.SemaphoreType.DMA((second,)),
            pltpu.SemaphoreType.DMA((second,)),
            pltpu.VMEM((rank, extent), jnp.float32),
            pltpu.SemaphoreType.DMA,
            *reduce_scratch,
            *reduce_scratch,
        ],
        compiler_params=pltpu.CompilerParams(collective_id=0, has_side_effects=True, vmem_limit_bytes=GRANT),
    )(field, start)


def in_hbm(x):
    return pltpu.with_memory_space_constraint(x, pltpu.HBM)


def local(nx, ny, nz, species_field, start_first, start_second):
    depth, rows, columns = species_field.shape
    rank, extent = start_first.shape[1], start_second.shape[0]
    species, ranks = S // nx, rank // ny
    cells = LANES // species
    fits = (
        columns % (nx * LANES) == 0
        and columns // nx == extent
        and nx * rows == extent
        and species == ny
        and extent % LANES == 0
        and nx * rows % LANES == 0
        and ranks % 8 == 0
    )
    if not fits:
        return local_general(nx, ny, nz, species_field, start_first, start_second)
    axes, sizes = ("gz", "gy", "gx"), (nz, ny, nx)
    factor_first, rows_second, gram_second = stages(in_hbm(species_field), in_hbm(start_first.T), axes, sizes, cells)
    rows_second = rows_second.reshape(species * depth * ranks, extent)
    factor_first, factor_second, core = pl.pallas_call(
        second_power_kernel,
        out_shape=(
            jax.ShapeDtypeStruct((rank, extent), jnp.float32),
            jax.ShapeDtypeStruct((rank, extent), jnp.float32),
            jax.ShapeDtypeStruct((rows_second.shape[0], rank), jnp.float32),
        ),
        in_specs=[VMEM, VMEM, VMEM, VMEM],
        out_specs=(VMEM, VMEM, VMEM),
        compiler_params=pltpu.CompilerParams(vmem_limit_bytes=GRANT),
    )(gram_second, start_second.T, rows_second, factor_first)
    return (factor_first.T, factor_second.T, core.reshape(species, depth, ranks, rank))


def solution(mesh):
    return jax.shard_map(
        functools.partial(local, mesh.shape["gx"], mesh.shape["gy"], mesh.shape["gz"]),
        mesh=mesh,
        in_specs=(P("gz", "gx", "gy"), P(), P()),
        out_specs=(P(), P(), P("gx", "gz", "gy", None)),
        check_vma=False,
    )
```

```python
import functools

import jax
import jax.numpy as jnp
from jax import lax
from jax.experimental import pallas as pl
from jax.experimental.pallas import tpu as pltpu
from jax.sharding import PartitionSpec as P

S = 16
ITERS = 2
PANEL = 32
LANES = 128
GRANT = 32 * 2**20
MESH = pl.DeviceIdType.MESH
VMEM = pl.BlockSpec(memory_space=pltpu.VMEM)

exact_precision = lax.Precision.HIGHEST


def dot_dims(a, b, contract_a, contract_b):
    return lax.dot_general(
        a, b, (((contract_a,), (contract_b,)), ((), ())),
        precision=exact_precision, preferred_element_type=jnp.float32,
    )


def partners(n, me):
    if n == 4:
        return [3 - me, lax.rem(me + 2, 4), me + 1 - 2 * lax.rem(me, 2)]
    return [lax.rem(me + d, n) for d in range(1, n)]


def send(src, dst, send_sem, recv_sem, target):
    copy = pltpu.make_async_remote_copy(
        src_ref=src, dst_ref=dst, send_sem=send_sem, recv_sem=recv_sem,
        device_id=target, device_id_type=MESH,
    )
    copy.start()
    return copy


def say_hello(targets):
    barrier = pltpu.get_barrier_semaphore()
    for target in targets:
        pl.semaphore_signal(barrier, inc=1, device_id=target, device_id_type=MESH)


def hear_hello(targets):
    pl.semaphore_wait(pltpu.get_barrier_semaphore(), len(targets))


def greet(targets):
    say_hello(targets)
    hear_hello(targets)


def axis_peers(axes, sizes):
    return [{axis: p} for axis, n in zip(axes, sizes) for p in partners(n, lax.axis_index(axis))]


def reduce_blocks(axes, sizes, splits, x_ref, o_ref, scratch):
    levels = len(axes)
    landing, totals = scratch[:levels], scratch[levels : 2 * levels - 1]
    send_sems, recv_sems = scratch[2 * levels - 1 :]
    me = [lax.axis_index(axis) for axis in axes]
    peers = [partners(n, m) for n, m in zip(sizes, me)]
    spot = [m if split > 1 else 0 for m, split in zip(me, splits)]
    sem = 0
    held = x_ref
    for level in range(levels):
        axis, n, split = axes[level], sizes[level], splits[level]
        land = landing[level]
        copies = []
        for p in peers[level]:
            src = held.at[p] if split > 1 else held.at[0]
            copies.append(send(src, land.at[me[level]], send_sems.at[sem], recv_sems.at[sem], {axis: p}))
            sem += 1
        land[me[level]] = held[spot[level]]
        for copy in copies:
            copy.wait()
        total = land[0]
        for source in range(1, n):
            total = total + land[source]
        if level < levels - 1:
            totals[level][...] = total
            held = totals[level]
        else:
            o_ref[tuple(spot)] = total

    for level in reversed(range(levels)):
        if splits[level] == 1:
            continue
        block = o_ref.at[tuple(spot[: level + 1])]
        copies = []
        for p in peers[level]:
            copies.append(send(block, block, send_sems.at[sem], recv_sems.at[sem], {axes[level]: p}))
            sem += 1
        for copy in copies:
            copy.wait()


def all_reduce_kernel(axes, sizes, splits, x_ref, o_ref, *scratch):
    greet(axis_peers(axes, sizes))
    reduce_blocks(axes, sizes, splits, x_ref, o_ref, scratch)


def reduce_plan(rows, columns, sizes):
    splits = []
    for n in sizes:
        splits.append(n if rows % n == 0 else 1)
        rows //= splits[-1]
    scratch = [
        pltpu.VMEM((n, *splits[level + 1 :], rows, columns), jnp.float32)
        for level, n in enumerate(sizes)
    ]
    scratch += [pltpu.VMEM((*splits[level + 1 :], rows, columns), jnp.float32) for level in range(len(sizes) - 1)]
    count = sum(n - 1 for n in sizes) + sum(n - 1 for n, split in zip(sizes, splits) if split > 1)
    scratch += [pltpu.SemaphoreType.DMA((count,)), pltpu.SemaphoreType.DMA((count,))]
    return splits, (*splits, rows, columns), scratch


def all_reduce(x, axes, sizes, collective_id):
    splits, blocked, scratch = reduce_plan(*x.shape, sizes)
    out = pl.pallas_call(
        functools.partial(all_reduce_kernel, axes, sizes, splits),
        out_shape=jax.ShapeDtypeStruct(blocked, jnp.float32),
        in_specs=[VMEM],
        out_specs=VMEM,
        scratch_shapes=scratch,
        compiler_params=pltpu.CompilerParams(collective_id=collective_id, has_side_effects=True),
    )(x.reshape(blocked))
    return out.reshape(x.shape)


def fibres_kernel(n, x_ref, o_ref, send_sems, recv_sems):
    me = lax.axis_index("gx")
    depth, rows, width = x_ref.shape[0], x_ref.shape[1], o_ref.shape[-1]
    peers = partners(n, me)
    greet([{"gx": p} for p in peers])
    copies = []
    for turn, p in enumerate(peers):
        columns = pl.ds(pl.multiple_of(p * width, width), width)
        copies.append(
            send(x_ref.at[:, :, columns], o_ref.at[:, me], send_sems.at[turn], recv_sems.at[turn], {"gx": p})
        )
    own = pl.ds(pl.multiple_of(me * width, width), width)
    for level in range(depth):
        o_ref[level, me] = x_ref[level, :, own]
    for copy in copies:
        copy.wait()


def gather_fibres(field, n):
    depth, rows, columns = field.shape
    width = columns // n
    if width % 128:
        return lax.all_to_all(field, "gx", split_axis=2, concat_axis=1, tiled=True)
    out = pl.pallas_call(
        functools.partial(fibres_kernel, n),
        out_shape=jax.ShapeDtypeStruct((depth, n, rows, width), jnp.float32),
        in_specs=[VMEM],
        out_specs=VMEM,
        scratch_shapes=[pltpu.SemaphoreType.DMA((n - 1,)), pltpu.SemaphoreType.DMA((n - 1,))],
        compiler_params=pltpu.CompilerParams(collective_id=0, has_side_effects=True),
    )(field)
    return out.reshape(depth, n * rows, width)


def exchange_kernel(nx, ny, x_ref, o_ref, send_sems, recv_sems):
    mx, my = lax.axis_index("gx"), lax.axis_index("gy")
    peers = [(px, my) for px in partners(nx, mx)]
    for py in partners(ny, my):
        peers += [(px, py) for px in partners(nx, mx) + [mx]]
    greet([{"gx": px, "gy": py} for px, py in peers])
    copies = []
    for turn, (px, py) in enumerate(peers):
        copies.append(
            send(x_ref.at[py, px], o_ref.at[my, mx], send_sems.at[turn], recv_sems.at[turn], {"gx": px, "gy": py})
        )
    o_ref[my, mx] = x_ref[my, mx]
    for copy in copies:
        copy.wait()


def exchange(blocks):
    ny, nx = blocks.shape[:2]
    count = nx * ny - 1
    return pl.pallas_call(
        functools.partial(exchange_kernel, nx, ny),
        out_shape=jax.ShapeDtypeStruct(blocks.shape, jnp.float32),
        in_specs=[VMEM],
        out_specs=VMEM,
        scratch_shapes=[pltpu.SemaphoreType.DMA((count,)), pltpu.SemaphoreType.DMA((count,))],
        compiler_params=pltpu.CompilerParams(collective_id=1, has_side_effects=True),
    )(blocks)


def inverse_lower(cross):
    rank = cross.shape[0]
    panel = next(size for size in (PANEL, 24, 8) if rank % size == 0)
    groups = panel // 8
    row = lax.broadcasted_iota(jnp.int32, (rank, rank), 0)
    column = lax.broadcasted_iota(jnp.int32, (rank, rank), 1)
    rest = cross
    rest_inverse = jnp.where(row == column, 1.0, 0.0).astype(jnp.float32)
    local_row = lax.broadcasted_iota(jnp.int32, (8, rank), 0)

    def spread(block, r):
        return jnp.broadcast_to(block[r : r + 1], (8, rank))

    done = []
    for start in range(0, rank, panel):
        upper = [rest[8 * g : 8 * g + 8] for g in range(groups)]
        inverse = [rest_inverse[8 * g : 8 * g + 8] for g in range(groups)]
        columns = {
            (j, g): jnp.broadcast_to(upper[g][:, start + j : start + j + 1], (8, rank))
            for j in range(panel) for g in range(j // 8, groups)
        }
        diagonal = [jnp.ones((8, rank), jnp.float32)] * groups
        for j in range(panel):
            own, r = divmod(j, 8)
            pivot = spread(columns[j, own], r)
            diagonal[own] = jnp.where(local_row == r, pivot, diagonal[own])
            if j == panel - 1:
                break
            reciprocal = 1.0 / pivot
            factor = {g: columns[j, g] * reciprocal for g in range(own, groups)}
            factor[own] = jnp.where(local_row > r, factor[own], 0.0)
            for other in range(j + 1, panel):
                value = spread(columns[j, other // 8], other % 8)
                for g in range(other // 8, groups):
                    columns[other, g] = columns[other, g] - factor[g] * value
            upper_row, inverse_row = spread(upper[own], r), spread(inverse[own], r)
            for g in range(own if r < 7 else own + 1, groups):
                upper[g] = upper[g] - factor[g] * upper_row
                inverse[g] = inverse[g] - factor[g] * inverse_row
        done += [inverse[g] * (1.0 / jnp.sqrt(diagonal[g])) for g in range(groups)]
        if start + panel < rank:
            scaled = jnp.concatenate([upper[g] / diagonal[g] for g in range(groups)], axis=0)
            both = jnp.concatenate([jnp.concatenate(upper, axis=0), jnp.concatenate(inverse, axis=0)], axis=1)
            update = dot_dims(scaled, both, 0, 0)
            after = start + panel
            rest = rest[panel:] - update[after:, :rank]
            rest_inverse = rest_inverse[panel:] - update[after:, rank:]
    return jnp.concatenate(done, axis=0)


def power_general_kernel(gram_ref, start_ref, out_ref):
    current = start_ref[...]
    for turn in range(ITERS):
        images = dot_dims(gram_ref[...], current, 1, 0)
        cross = dot_dims(images, images, 0, 0)
        current = dot_dims(images, inverse_lower(cross), 1, 1)
    out_ref[...] = current


def leading(gram, start):
    return pl.pallas_call(
        power_general_kernel,
        out_shape=jax.ShapeDtypeStruct(start.shape, jnp.float32),
        in_specs=[VMEM, VMEM],
        out_specs=VMEM,
    )(gram, start)


def local_general(nx, ny, nz, species_field, start_first, start_second):
    axes, sizes = ("gz", "gy", "gx"), (nz, ny, nx)
    fibres = gather_fibres(species_field, nx)
    partial_gram = jnp.einsum("zic,zjc->ij", fibres, fibres, precision=exact_precision)
    gram_first = all_reduce(partial_gram, axes, sizes, 2)
    factor_first = leading(gram_first, start_first)

    depth = fibres.shape[0]
    cells = fibres.shape[2] // S
    rank = start_first.shape[1]
    species, ranks = S // nx, rank // ny
    projected = jnp.einsum("zim,ir->zmr", fibres, factor_first, precision=exact_precision)
    blocks = projected.reshape(depth, cells, nx, species, ny, ranks)
    blocks = blocks.transpose(4, 2, 1, 3, 0, 5).reshape(ny, nx, cells, species * depth * ranks)
    columns = exchange(blocks)
    columns = columns.reshape(ny * nx * cells, species * depth * ranks)
    partial_second = dot_dims(columns, columns, 1, 1)
    gram_second = all_reduce(partial_second, axes, sizes, 3)
    factor_second = leading(gram_second, start_second)
    core = dot_dims(columns, factor_second, 0, 0)
    core = core.reshape(species, depth, ranks, factor_second.shape[1])
    return (factor_first, factor_second, core)


def upper_blocks(count):
    return [(a, b) for a in range(count) for b in range(a, count)]


def add_gram(gram_ref, parts, contract, first):
    for slot, (a, b) in enumerate(upper_blocks(len(parts))):
        block = pl.ds(slot * LANES, LANES)
        term = dot_dims(parts[a], parts[b], contract, contract)
        gram_ref[block, :] = term if first else gram_ref[block, :] + term


def times_gram(current, gram_ref):
    count = current.shape[1] // LANES
    sums = [None] * count
    for slot, (a, b) in enumerate(upper_blocks(count)):
        block = gram_ref[slot * LANES : (slot + 1) * LANES, :]
        terms = [(b, a, 0)] if a == b else [(b, a, 0), (a, b, 1)]
        for to, of, contract in terms:
            term = dot_dims(current[:, of * LANES : (of + 1) * LANES], block, 1, contract)
            sums[to] = term if sums[to] is None else sums[to] + term
    return jnp.concatenate(sums, axis=1)


def power_steps(gram_ref, current):
    for turn in range(ITERS):
        images = times_gram(current, gram_ref)
        cross = dot_dims(images, images, 1, 1)
        current = dot_dims(inverse_lower(cross), images, 1, 0)
    return current


def second_power_kernel(gram_ref, start_ref, rows_ref, first_ref, first_out_ref, out_ref, core_ref):
    first_out_ref[...] = first_ref[...]
    current = power_steps(gram_ref, start_ref[...])
    out_ref[...] = current
    core_ref[...] = dot_dims(rows_ref[...], current, 1, 1)


def species_major(block, order):
    high = block.astype(jnp.bfloat16)
    left = block - high.astype(jnp.float32)
    middle = left.astype(jnp.bfloat16)
    low = (left - middle.astype(jnp.float32)).astype(jnp.bfloat16)
    moved = [
        lax.dot_general(part, order, (((1,), (0,)), ((), ())), preferred_element_type=jnp.float32)
        for part in (high, middle, low)
    ]
    return (moved[0] + moved[1]) + moved[2]


def first_exchange(n, targets, x_ref, start_load, field, fibres, gram, packed, load_sems, send_sems, recv_sems):
    me = lax.axis_index("gx")
    depth, rows, columns = field.shape
    span = n * LANES
    cells = span // S
    width = columns // n
    loads = [pltpu.make_async_copy(x_ref.at[z], field.at[z], load_sems.at[z]) for z in range(depth)]
    for load in loads + [start_load]:
        load.start()
    say_hello(targets)
    peers = partners(n, me)
    source = lax.broadcasted_iota(jnp.int32, (span, span), 0)
    target = lax.broadcasted_iota(jnp.int32, (span, span), 1)
    species = lax.shift_right_logical(target, cells.bit_length() - 1)
    order = jnp.where(source == (target & (cells - 1)) * S + species, 1.0, 0.0).astype(jnp.bfloat16)
    copies = []
    for level in range(depth):
        loads[level].wait()
        for chunk in range(columns // span):
            moved = species_major(field[level, :, chunk * span : (chunk + 1) * span], order)
            lanes = pl.ds(chunk * LANES, LANES)
            for p in range(n):
                packed[level, p, :, lanes] = moved[:, p * LANES : (p + 1) * LANES]
        if level == 0:
            hear_hello(targets)
        turns = list(enumerate(peers))
        if level > 0:
            turns = turns[-1:] + turns[:-1]
        for turn, p in turns:
            sem = level * (n - 1) + turn
            copies.append(
                send(packed.at[level, p], fibres.at[level, me], send_sems.at[sem], recv_sems.at[sem], {"gx": p})
            )
        fibres[level, me] = packed[level, me]
    for level in range(depth):
        for copy in copies[level * (n - 1) : (level + 1) * (n - 1)]:
            copy.wait()
        whole = fibres[level].reshape(n * rows, width)
        parts = [whole[a : a + LANES] for a in range(0, n * rows, LANES)]
        add_gram(gram, parts, 1, level == 0)
    start_load.wait()


def second_exchange(n, cells, factor, fibres, rows_ref, gram, packed, land, send_sems, recv_sems):
    me = lax.axis_index("gy")
    depth, ranks, width = packed.shape[0], packed.shape[2], packed.shape[3]
    peers = partners(n, me)
    copies = []
    for level in range(depth):
        whole = fibres[level].reshape(factor.shape[1], width)
        packed[level] = dot_dims(factor, whole, 1, 0).reshape(n, ranks, width)
        for turn, p in enumerate(peers):
            sem = level * (n - 1) + turn
            copies.append(
                send(packed.at[level, p], land.at[me, level], send_sems.at[sem], recv_sems.at[sem], {"gy": p})
            )
        land[me, level] = packed[level, me]
    lane_group = lax.shift_right_logical(
        lax.broadcasted_iota(jnp.int32, (ranks, LANES), 1), cells.bit_length() - 1
    )
    for level in range(depth):
        for copy in copies[level * (n - 1) : (level + 1) * (n - 1)]:
            copy.wait()
        chunks = width // LANES
        for tile in range(chunks):
            for s in range(n):
                merged = None
                for g in range(n):
                    t, chunk = divmod(n * tile + g, chunks)
                    turned = land[t, level, :, chunk * LANES : (chunk + 1) * LANES]
                    if g != s:
                        turned = pltpu.roll(turned, cells * ((g - s) % n), 1)
                    merged = turned if g == 0 else jnp.where(lane_group == g, turned, merged)
                rows_ref[s, level, :, tile * LANES : (tile + 1) * LANES] = merged
        whole = rows_ref[:, level].reshape(n * ranks, width)
        parts = [whole[:, a : a + LANES] for a in range(0, width, LANES)]
        add_gram(gram, parts, 0, level == 0)


def flat_targets(nx, ny, nz):
    mx, my, mz = lax.axis_index("gx"), lax.axis_index("gy"), lax.axis_index("gz")
    targets = [{"gz": p} for p in partners(nz, mz)]
    for px in partners(nx, mx) + [mx]:
        targets += [{"gx": px, "gy": py} for py in partners(ny, my)]
        if px is not mx:
            targets.append({"gx": px})
    return targets


def flat_plan(rows, nx, ny, nz):
    piece = rows // (nx * ny * nz)
    count = nx * (nz - 1) + nx * ny - 1
    return (nz, nx, ny, piece, LANES), [
        pltpu.VMEM((nz - 1, nx, ny, piece, LANES), jnp.float32),
        pltpu.VMEM((nx, ny, piece, LANES), jnp.float32),
        pltpu.VMEM((nx, ny, piece, LANES), jnp.float32),
        pltpu.VMEM((nz, nx, ny, piece, LANES), jnp.float32),
        pltpu.SemaphoreType.DMA((2, count)),
        pltpu.SemaphoreType.DMA((2, count)),
    ]


def flat_reduce(nx, ny, nz, held, scratch):
    land_core, half, land, total, send_sems, recv_sems = scratch
    mx, my, mz = lax.axis_index("gx"), lax.axis_index("gy"), lax.axis_index("gz")
    cores, columns, planes = partners(nz, mz), partners(nx, mx), partners(ny, my)
    groups = columns + [mx]
    base = nx * (nz - 1)

    def turns(px):
        return [(px, py) for py in planes + ([] if px is mx else [my])]

    order = [(i, px, py) for i, (px, py) in enumerate(sum((turns(px) for px in groups), []))]

    across = []
    for i, px in enumerate(groups):
        across.append([
            send(held.at[p, px], land_core.at[d, px], send_sems.at[0, i * (nz - 1) + d],
                 recv_sems.at[0, i * (nz - 1) + d], {"gz": p})
            for d, p in enumerate(cores)
        ])
    copies = {}
    for i, px in enumerate(groups):
        for copy in across[i]:
            copy.wait()
        summed = held[mz, px]
        for d in range(nz - 1):
            summed = summed + land_core[d, px]
        half[px] = summed
        for slot, qx, qy in order:
            if qx is px:
                copies[slot] = send(half.at[qx, qy], land.at[mx, my], send_sems.at[0, base + slot],
                                    recv_sems.at[0, base + slot], {"gx": qx, "gy": qy})
    result = half[mx, my]
    for slot, qx, qy in reversed(order):
        copies[slot].wait()
        result = result + land[qx, qy]
    total[mz, mx, my] = result
    own = total.at[mz, mx, my]
    for slot, qx, qy in order:
        copies[slot] = send(own, own, send_sems.at[1, base + slot], recv_sems.at[1, base + slot], {"gx": qx, "gy": qy})
    across = []
    for i, px in reversed(list(enumerate(groups))):
        for slot, qx, qy in order:
            if qx is px:
                copies[slot].wait()
        block = total.at[mz, px]
        for d, p in enumerate(cores):
            across.append(send(block, block, send_sems.at[1, i * (nz - 1) + d], recv_sems.at[1, i * (nz - 1) + d], {"gz": p}))
    for copy in across:
        copy.wait()


def stages_kernel(axes, sizes, cells, x_ref, start_ref, factor_ref, rows_ref, gram_ref, *scratch):
    nz, ny, nx = sizes
    targets = flat_targets(nx, ny, nz)
    gram, field, fibres, packed, load_sems, send_first, recv_first = scratch[:7]
    packed_second, land, send_second, recv_second, start, start_sem = scratch[7:13]
    half = (len(scratch) - 13) // 2
    reduces = scratch[13 : 13 + half], scratch[13 + half :]
    start_load = pltpu.make_async_copy(start_ref, start, start_sem)

    def reduced(reduce_scratch, into):
        held, total = reduce_scratch[0], reduce_scratch[4]
        held[...] = gram[...].reshape(held.shape)
        flat_reduce(nx, ny, nz, held, reduce_scratch[1:])
        into[...] = total[...].reshape(into.shape)

    first_exchange(nx, targets, x_ref, start_load, field, fibres, gram, packed, load_sems, send_first, recv_first)
    reduced(reduces[0], gram)
    factor = power_steps(gram, start[...])
    factor_ref[...] = factor
    second_exchange(ny, cells, factor, fibres, rows_ref, gram, packed_second, land, send_second, recv_second)
    reduced(reduces[1], gram_ref)


def stages(field, start, axes, sizes, cells):
    nz, ny, nx = sizes
    depth, rows, columns = field.shape
    rank, extent = start.shape
    width = columns // nx
    ranks = rank // ny
    gram_shape = (len(upper_blocks(extent // LANES)) * LANES, LANES)
    blocked, reduce_scratch = flat_plan(gram_shape[0], nx, ny, nz)
    reduce_scratch = [pltpu.VMEM(blocked, jnp.float32)] + reduce_scratch
    first, second = depth * (nx - 1), depth * (ny - 1)
    return pl.pallas_call(
        functools.partial(stages_kernel, axes, sizes, cells),
        out_shape=(
            jax.ShapeDtypeStruct((rank, extent), jnp.float32),
            jax.ShapeDtypeStruct((ny, depth, ranks, width), jnp.float32),
            jax.ShapeDtypeStruct(gram_shape, jnp.float32),
        ),
        in_specs=[pl.BlockSpec(memory_space=pltpu.HBM)] * 2,
        out_specs=(VMEM, VMEM, VMEM),
        scratch_shapes=[
            pltpu.VMEM(gram_shape, jnp.float32),
            pltpu.VMEM((depth, rows, columns), jnp.float32),
            pltpu.VMEM((depth, nx, rows, width), jnp.float32),
            pltpu.VMEM((depth, nx, rows, width), jnp.float32),
            pltpu.SemaphoreType.DMA((depth,)),
            pltpu.SemaphoreType.DMA((first,)),
            pltpu.SemaphoreType.DMA((first,)),
            pltpu.VMEM((depth, ny, ranks, width), jnp.float32),
            pltpu.VMEM((ny, depth, ranks, width), jnp.float32),
            pltpu.SemaphoreType.DMA((second,)),
            pltpu.SemaphoreType.DMA((second,)),
            pltpu.VMEM((rank, extent), jnp.float32),
            pltpu.SemaphoreType.DMA,
            *reduce_scratch,
            *reduce_scratch,
        ],
        compiler_params=pltpu.CompilerParams(collective_id=0, has_side_effects=True, vmem_limit_bytes=GRANT),
    )(field, start)


def in_hbm(x):
    return pltpu.with_memory_space_constraint(x, pltpu.HBM)


def local(nx, ny, nz, species_field, start_first, start_second):
    depth, rows, columns = species_field.shape
    rank, extent = start_first.shape[1], start_second.shape[0]
    species, ranks = S // nx, rank // ny
    cells = LANES // species
    fits = (
        columns % (nx * LANES) == 0
        and columns // nx == extent
        and nx * rows == extent
        and species == ny
        and extent % LANES == 0
        and nx * rows % LANES == 0
        and ranks % 8 == 0
        and len(upper_blocks(extent // LANES)) * LANES % (8 * nx * ny * nz) == 0
    )
    if not fits:
        return local_general(nx, ny, nz, species_field, start_first, start_second)
    axes, sizes = ("gz", "gy", "gx"), (nz, ny, nx)
    factor_first, rows_second, gram_second = stages(in_hbm(species_field), in_hbm(start_first.T), axes, sizes, cells)
    rows_second = rows_second.reshape(species * depth * ranks, extent)
    factor_first, factor_second, core = pl.pallas_call(
        second_power_kernel,
        out_shape=(
            jax.ShapeDtypeStruct((rank, extent), jnp.float32),
            jax.ShapeDtypeStruct((rank, extent), jnp.float32),
            jax.ShapeDtypeStruct((rows_second.shape[0], rank), jnp.float32),
        ),
        in_specs=[VMEM, VMEM, VMEM, VMEM],
        out_specs=(VMEM, VMEM, VMEM),
        compiler_params=pltpu.CompilerParams(vmem_limit_bytes=GRANT),
    )(gram_second, start_second.T, rows_second, factor_first)
    return (factor_first.T, factor_second.T, core.reshape(species, depth, ranks, rank))


def solution(mesh):
    return jax.shard_map(
        functools.partial(local, mesh.shape["gx"], mesh.shape["gy"], mesh.shape["gz"]),
        mesh=mesh,
        in_specs=(P("gz", "gx", "gy"), P(), P()),
        out_specs=(P(), P(), P("gx", "gz", "gy", None)),
        check_vma=False,
    )
```

```python
import functools

import jax
import jax.numpy as jnp
from jax import lax
from jax.experimental import pallas as pl
from jax.experimental.pallas import tpu as pltpu
from jax.sharding import PartitionSpec as P

S = 16
ITERS = 2
LANES = 128
GRANT = 32 * 2**20
MESH = pl.DeviceIdType.MESH
VMEM = pl.BlockSpec(memory_space=pltpu.VMEM)

exact_precision = lax.Precision.HIGHEST


def dot_dims(a, b, contract_a, contract_b):
    return lax.dot_general(
        a, b, (((contract_a,), (contract_b,)), ((), ())),
        precision=exact_precision, preferred_element_type=jnp.float32,
    )


def partners(n, me):
    if n == 4:
        return [3 - me, lax.rem(me + 2, 4), me + 1 - 2 * lax.rem(me, 2)]
    return [lax.rem(me + d, n) for d in range(1, n)]


def send(src, dst, send_sem, recv_sem, target):
    copy = pltpu.make_async_remote_copy(
        src_ref=src, dst_ref=dst, send_sem=send_sem, recv_sem=recv_sem,
        device_id=target, device_id_type=MESH,
    )
    copy.start()
    return copy


def say_hello(targets):
    barrier = pltpu.get_barrier_semaphore()
    for target in targets:
        pl.semaphore_signal(barrier, inc=1, device_id=target, device_id_type=MESH)


def hear_hello(targets):
    pl.semaphore_wait(pltpu.get_barrier_semaphore(), len(targets))


def greet(targets):
    say_hello(targets)
    hear_hello(targets)


def axis_peers(axes, sizes):
    return [{axis: p} for axis, n in zip(axes, sizes) for p in partners(n, lax.axis_index(axis))]


def reduce_blocks(axes, sizes, splits, x_ref, o_ref, scratch):
    levels = len(axes)
    landing, totals = scratch[:levels], scratch[levels : 2 * levels - 1]
    send_sems, recv_sems = scratch[2 * levels - 1 :]
    me = [lax.axis_index(axis) for axis in axes]
    peers = [partners(n, m) for n, m in zip(sizes, me)]
    spot = [m if split > 1 else 0 for m, split in zip(me, splits)]
    sem = 0
    held = x_ref
    for level in range(levels):
        axis, n, split = axes[level], sizes[level], splits[level]
        land = landing[level]
        copies = []
        for p in peers[level]:
            src = held.at[p] if split > 1 else held.at[0]
            copies.append(send(src, land.at[me[level]], send_sems.at[sem], recv_sems.at[sem], {axis: p}))
            sem += 1
        land[me[level]] = held[spot[level]]
        for copy in copies:
            copy.wait()
        total = land[0]
        for source in range(1, n):
            total = total + land[source]
        if level < levels - 1:
            totals[level][...] = total
            held = totals[level]
        else:
            o_ref[tuple(spot)] = total

    for level in reversed(range(levels)):
        if splits[level] == 1:
            continue
        block = o_ref.at[tuple(spot[: level + 1])]
        copies = []
        for p in peers[level]:
            copies.append(send(block, block, send_sems.at[sem], recv_sems.at[sem], {axes[level]: p}))
            sem += 1
        for copy in copies:
            copy.wait()


def all_reduce_kernel(axes, sizes, splits, x_ref, o_ref, *scratch):
    greet(axis_peers(axes, sizes))
    reduce_blocks(axes, sizes, splits, x_ref, o_ref, scratch)


def reduce_plan(rows, columns, sizes):
    splits = []
    for n in sizes:
        splits.append(n if rows % n == 0 else 1)
        rows //= splits[-1]
    scratch = [
        pltpu.VMEM((n, *splits[level + 1 :], rows, columns), jnp.float32)
        for level, n in enumerate(sizes)
    ]
    scratch += [pltpu.VMEM((*splits[level + 1 :], rows, columns), jnp.float32) for level in range(len(sizes) - 1)]
    count = sum(n - 1 for n in sizes) + sum(n - 1 for n, split in zip(sizes, splits) if split > 1)
    scratch += [pltpu.SemaphoreType.DMA((count,)), pltpu.SemaphoreType.DMA((count,))]
    return splits, (*splits, rows, columns), scratch


def all_reduce(x, axes, sizes, collective_id):
    splits, blocked, scratch = reduce_plan(*x.shape, sizes)
    out = pl.pallas_call(
        functools.partial(all_reduce_kernel, axes, sizes, splits),
        out_shape=jax.ShapeDtypeStruct(blocked, jnp.float32),
        in_specs=[VMEM],
        out_specs=VMEM,
        scratch_shapes=scratch,
        compiler_params=pltpu.CompilerParams(collective_id=collective_id, has_side_effects=True),
    )(x.reshape(blocked))
    return out.reshape(x.shape)


def fibres_kernel(n, x_ref, o_ref, send_sems, recv_sems):
    me = lax.axis_index("gx")
    depth, rows, width = x_ref.shape[0], x_ref.shape[1], o_ref.shape[-1]
    peers = partners(n, me)
    greet([{"gx": p} for p in peers])
    copies = []
    for turn, p in enumerate(peers):
        columns = pl.ds(pl.multiple_of(p * width, width), width)
        copies.append(
            send(x_ref.at[:, :, columns], o_ref.at[:, me], send_sems.at[turn], recv_sems.at[turn], {"gx": p})
        )
    own = pl.ds(pl.multiple_of(me * width, width), width)
    for level in range(depth):
        o_ref[level, me] = x_ref[level, :, own]
    for copy in copies:
        copy.wait()


def gather_fibres(field, n):
    depth, rows, columns = field.shape
    width = columns // n
    if width % 128:
        return lax.all_to_all(field, "gx", split_axis=2, concat_axis=1, tiled=True)
    out = pl.pallas_call(
        functools.partial(fibres_kernel, n),
        out_shape=jax.ShapeDtypeStruct((depth, n, rows, width), jnp.float32),
        in_specs=[VMEM],
        out_specs=VMEM,
        scratch_shapes=[pltpu.SemaphoreType.DMA((n - 1,)), pltpu.SemaphoreType.DMA((n - 1,))],
        compiler_params=pltpu.CompilerParams(collective_id=0, has_side_effects=True),
    )(field)
    return out.reshape(depth, n * rows, width)


def exchange_kernel(nx, ny, x_ref, o_ref, send_sems, recv_sems):
    mx, my = lax.axis_index("gx"), lax.axis_index("gy")
    peers = [(px, my) for px in partners(nx, mx)]
    for py in partners(ny, my):
        peers += [(px, py) for px in partners(nx, mx) + [mx]]
    greet([{"gx": px, "gy": py} for px, py in peers])
    copies = []
    for turn, (px, py) in enumerate(peers):
        copies.append(
            send(x_ref.at[py, px], o_ref.at[my, mx], send_sems.at[turn], recv_sems.at[turn], {"gx": px, "gy": py})
        )
    o_ref[my, mx] = x_ref[my, mx]
    for copy in copies:
        copy.wait()


def exchange(blocks):
    ny, nx = blocks.shape[:2]
    count = nx * ny - 1
    return pl.pallas_call(
        functools.partial(exchange_kernel, nx, ny),
        out_shape=jax.ShapeDtypeStruct(blocks.shape, jnp.float32),
        in_specs=[VMEM],
        out_specs=VMEM,
        scratch_shapes=[pltpu.SemaphoreType.DMA((count,)), pltpu.SemaphoreType.DMA((count,))],
        compiler_params=pltpu.CompilerParams(collective_id=1, has_side_effects=True),
    )(blocks)


def inverse_lower(cross):
    rank = cross.shape[0]
    groups = rank // 8
    local_row = lax.broadcasted_iota(jnp.int32, (8, rank), 0)
    lane = lax.broadcasted_iota(jnp.int32, (8, rank), 1)

    def row_of(block, r):
        return jnp.broadcast_to(block[r : r + 1], (8, rank))

    def column_of(block, c):
        return jnp.broadcast_to(block[:, c : c + 1], (8, rank))

    rest = [cross[8 * g : 8 * g + 8] for g in range(groups)]
    inverse = [jnp.where(lane == local_row + 8 * g, 1.0, 0.0).astype(jnp.float32) for g in range(groups)]
    pivots = [column_of(rest[0], j) for j in range(8)]
    near = [column_of(rest[1], j) for j in range(8)] if groups > 1 else None
    done = []
    for k in range(groups):
        low = 8 * k
        next_pivots = [column_of(rest[k + 1], low + 8 + j) for j in range(8)] if k + 1 < groups else None
        next_near = [column_of(rest[k + 2], low + 8 + j) for j in range(8)] if k + 2 < groups else None
        columns = {(j, k + 1): near[j] for j in range(8)} if k + 1 < groups else {}
        for g in range(k + 2, groups):
            for j in range(8):
                columns[j, g] = column_of(rest[g], low + j)
        diagonal = jnp.ones((8, rank), jnp.float32)
        factors = []
        for j in range(8):
            pivot = row_of(pivots[j], j)
            diagonal = jnp.where(local_row == j, pivot, diagonal)
            reciprocal = 1.0 / pivot
            factor = pivots[j] * reciprocal
            factors.append(factor)
            values = {other: row_of(pivots[j], other) for other in range(j + 1, 8)}
            for other in range(j + 1, 8):
                if other == j + 1:
                    change = (pivots[j] * values[other]) * reciprocal
                else:
                    change = factor * values[other]
                pivots[other] = pivots[other] - change
            rest_row, inverse_row = row_of(rest[k], j), row_of(inverse[k], j)
            below = jnp.where(local_row > j, factor, 0.0)
            rest[k] = rest[k] - below * rest_row
            inverse[k] = inverse[k] - below * inverse_row
            if k + 1 < groups:
                ahead = [row_of(columns[j, k + 1], other) for other in range(8)]
            for g in range(k + 1, min(k + 3, groups)):
                factor = columns[j, g] * reciprocal
                for other in range(j + 1, 8):
                    columns[other, g] = columns[other, g] - factor * values[other]
                following = next_pivots if g == k + 1 else next_near
                for other in range(8):
                    following[other] = following[other] - factor * ahead[other]
                rest[g] = rest[g] - factor * rest_row
                inverse[g] = inverse[g] - factor * inverse_row
        done.append(inverse[k] * (1.0 / jnp.sqrt(diagonal)))
        if k + 3 < groups:
            reciprocal = 1.0 / diagonal
            solved, solved_inverse = rest[k] * reciprocal, inverse[k] * reciprocal
            for j in range(7, 0, -1):
                above = jnp.zeros((8, rank), jnp.float32)
                for i in range(j):
                    above = jnp.where(local_row == i, row_of(factors[i], j), above)
                solved = solved - above * row_of(solved, j)
                solved_inverse = solved_inverse - above * row_of(solved_inverse, j)
            for j in range(8):
                rest_row, inverse_row = row_of(solved, j), row_of(solved_inverse, j)
                for g in range(k + 3, groups):
                    rest[g] = rest[g] - columns[j, g] * rest_row
                    inverse[g] = inverse[g] - columns[j, g] * inverse_row
        pivots, near = next_pivots, next_near
    return jnp.concatenate(done, axis=0)


def power_general_kernel(gram_ref, start_ref, out_ref):
    current = start_ref[...]
    for turn in range(ITERS):
        images = dot_dims(gram_ref[...], current, 1, 0)
        cross = dot_dims(images, images, 0, 0)
        current = dot_dims(images, inverse_lower(cross), 1, 1)
    out_ref[...] = current


def leading(gram, start):
    return pl.pallas_call(
        power_general_kernel,
        out_shape=jax.ShapeDtypeStruct(start.shape, jnp.float32),
        in_specs=[VMEM, VMEM],
        out_specs=VMEM,
    )(gram, start)


def local_general(nx, ny, nz, species_field, start_first, start_second):
    axes, sizes = ("gz", "gy", "gx"), (nz, ny, nx)
    fibres = gather_fibres(species_field, nx)
    partial_gram = jnp.einsum("zic,zjc->ij", fibres, fibres, precision=exact_precision)
    gram_first = all_reduce(partial_gram, axes, sizes, 2)
    factor_first = leading(gram_first, start_first)

    depth = fibres.shape[0]
    cells = fibres.shape[2] // S
    rank = start_first.shape[1]
    species, ranks = S // nx, rank // ny
    projected = jnp.einsum("zim,ir->zmr", fibres, factor_first, precision=exact_precision)
    blocks = projected.reshape(depth, cells, nx, species, ny, ranks)
    blocks = blocks.transpose(4, 2, 1, 3, 0, 5).reshape(ny, nx, cells, species * depth * ranks)
    columns = exchange(blocks)
    columns = columns.reshape(ny * nx * cells, species * depth * ranks)
    partial_second = dot_dims(columns, columns, 1, 1)
    gram_second = all_reduce(partial_second, axes, sizes, 3)
    factor_second = leading(gram_second, start_second)
    core = dot_dims(columns, factor_second, 0, 0)
    core = core.reshape(species, depth, ranks, factor_second.shape[1])
    return (factor_first, factor_second, core)


def upper_blocks(count):
    return [(a, b) for a in range(count) for b in range(a, count)]


def add_gram(gram_ref, parts, contract, first):
    for slot, (a, b) in enumerate(upper_blocks(len(parts))):
        block = pl.ds(slot * LANES, LANES)
        term = dot_dims(parts[a], parts[b], contract, contract)
        gram_ref[block, :] = term if first else gram_ref[block, :] + term


def times_gram(current, gram_ref):
    count = current.shape[1] // LANES
    sums = [None] * count
    for slot, (a, b) in enumerate(upper_blocks(count)):
        block = gram_ref[slot * LANES : (slot + 1) * LANES, :]
        terms = [(b, a, 0)] if a == b else [(b, a, 0), (a, b, 1)]
        for to, of, contract in terms:
            term = dot_dims(current[:, of * LANES : (of + 1) * LANES], block, 1, contract)
            sums[to] = term if sums[to] is None else sums[to] + term
    return jnp.concatenate(sums, axis=1)


def power_steps(gram_ref, current):
    for turn in range(ITERS):
        images = times_gram(current, gram_ref)
        cross = dot_dims(images, images, 1, 1)
        current = dot_dims(inverse_lower(cross), images, 1, 0)
    return current


def second_power_kernel(gram_ref, start_ref, rows_ref, first_ref, first_out_ref, out_ref, core_ref):
    first_out_ref[...] = first_ref[...]
    current = power_steps(gram_ref, start_ref[...])
    out_ref[...] = current
    core_ref[...] = dot_dims(rows_ref[...], current, 1, 1)


def species_major(block, order):
    high = block.astype(jnp.bfloat16)
    left = block - high.astype(jnp.float32)
    middle = left.astype(jnp.bfloat16)
    low = (left - middle.astype(jnp.float32)).astype(jnp.bfloat16)
    moved = [
        lax.dot_general(part, order, (((1,), (0,)), ((), ())), preferred_element_type=jnp.float32)
        for part in (high, middle, low)
    ]
    return (moved[0] + moved[1]) + moved[2]


def first_exchange(n, targets, x_ref, start_load, field, fibres, gram, packed, load_sems, send_sems, recv_sems):
    me = lax.axis_index("gx")
    depth, rows, columns = field.shape
    span = n * LANES
    cells = span // S
    width = columns // n
    loads = [pltpu.make_async_copy(x_ref.at[z], field.at[z], load_sems.at[z]) for z in range(depth)]
    for load in loads + [start_load]:
        load.start()
    say_hello(targets)
    peers = partners(n, me)
    source = lax.broadcasted_iota(jnp.int32, (span, span), 0)
    target = lax.broadcasted_iota(jnp.int32, (span, span), 1)
    species = lax.shift_right_logical(target, cells.bit_length() - 1)
    order = jnp.where(source == (target & (cells - 1)) * S + species, 1.0, 0.0).astype(jnp.bfloat16)
    copies = []
    for level in range(depth):
        loads[level].wait()
        for chunk in range(columns // span):
            moved = species_major(field[level, :, chunk * span : (chunk + 1) * span], order)
            lanes = pl.ds(chunk * LANES, LANES)
            for p in range(n):
                packed[level, p, :, lanes] = moved[:, p * LANES : (p + 1) * LANES]
        if level == 0:
            hear_hello(targets)
        turns = list(enumerate(peers))
        if level > 0:
            turns = turns[-1:] + turns[:-1]
        for turn, p in turns:
            sem = level * (n - 1) + turn
            copies.append(
                send(packed.at[level, p], fibres.at[level, me], send_sems.at[sem], recv_sems.at[sem], {"gx": p})
            )
        fibres[level, me] = packed[level, me]
    for level in range(depth):
        for copy in copies[level * (n - 1) : (level + 1) * (n - 1)]:
            copy.wait()
        whole = fibres[level].reshape(n * rows, width)
        parts = [whole[a : a + LANES] for a in range(0, n * rows, LANES)]
        add_gram(gram, parts, 1, level == 0)
    start_load.wait()


def second_exchange(n, cells, factor, fibres, rows_ref, gram, packed, land, send_sems, recv_sems):
    me = lax.axis_index("gy")
    depth, ranks, width = packed.shape[0], packed.shape[2], packed.shape[3]
    peers = partners(n, me)
    copies = []
    for level in range(depth):
        whole = fibres[level].reshape(factor.shape[1], width)
        packed[level] = dot_dims(factor, whole, 1, 0).reshape(n, ranks, width)
        for turn, p in enumerate(peers):
            sem = level * (n - 1) + turn
            copies.append(
                send(packed.at[level, p], land.at[me, level], send_sems.at[sem], recv_sems.at[sem], {"gy": p})
            )
        land[me, level] = packed[level, me]
    lane_group = lax.shift_right_logical(
        lax.broadcasted_iota(jnp.int32, (ranks, LANES), 1), cells.bit_length() - 1
    )
    for level in range(depth):
        for copy in copies[level * (n - 1) : (level + 1) * (n - 1)]:
            copy.wait()
        chunks = width // LANES
        for tile in range(chunks):
            for s in range(n):
                merged = None
                for g in range(n):
                    t, chunk = divmod(n * tile + g, chunks)
                    turned = land[t, level, :, chunk * LANES : (chunk + 1) * LANES]
                    if g != s:
                        turned = pltpu.roll(turned, cells * ((g - s) % n), 1)
                    merged = turned if g == 0 else jnp.where(lane_group == g, turned, merged)
                rows_ref[s, level, :, tile * LANES : (tile + 1) * LANES] = merged
        whole = rows_ref[:, level].reshape(n * ranks, width)
        parts = [whole[:, a : a + LANES] for a in range(0, width, LANES)]
        add_gram(gram, parts, 0, level == 0)


def flat_targets(nx, ny, nz):
    mx, my, mz = lax.axis_index("gx"), lax.axis_index("gy"), lax.axis_index("gz")
    targets = [{"gz": p} for p in partners(nz, mz)]
    for px in partners(nx, mx) + [mx]:
        targets += [{"gx": px, "gy": py} for py in partners(ny, my)]
        if px is not mx:
            targets.append({"gx": px})
    return targets


def flat_plan(rows, nx, ny, nz):
    piece = rows // (nx * ny * nz)
    count = nx * (nz - 1) + nx * ny - 1
    return (nz, nx, ny, piece, LANES), [
        pltpu.VMEM((nz - 1, nx, ny, piece, LANES), jnp.float32),
        pltpu.VMEM((nx, ny, piece, LANES), jnp.float32),
        pltpu.VMEM((nx, ny, piece, LANES), jnp.float32),
        pltpu.VMEM((nz, nx, ny, piece, LANES), jnp.float32),
        pltpu.SemaphoreType.DMA((2, count)),
        pltpu.SemaphoreType.DMA((2, count)),
    ]


def flat_reduce(nx, ny, nz, held, scratch):
    land_core, half, land, total, send_sems, recv_sems = scratch
    mx, my, mz = lax.axis_index("gx"), lax.axis_index("gy"), lax.axis_index("gz")
    cores, columns, planes = partners(nz, mz), partners(nx, mx), partners(ny, my)
    groups = columns + [mx]
    base = nx * (nz - 1)

    def turns(px):
        return [(px, py) for py in planes + ([] if px is mx else [my])]

    order = [(i, px, py) for i, (px, py) in enumerate(sum((turns(px) for px in groups), []))]

    across = []
    for i, px in enumerate(groups):
        across.append([
            send(held.at[p, px], land_core.at[d, px], send_sems.at[0, i * (nz - 1) + d],
                 recv_sems.at[0, i * (nz - 1) + d], {"gz": p})
            for d, p in enumerate(cores)
        ])
    copies = {}
    for i, px in enumerate(groups):
        for copy in across[i]:
            copy.wait()
        summed = held[mz, px]
        for d in range(nz - 1):
            summed = summed + land_core[d, px]
        half[px] = summed
        for slot, qx, qy in order:
            if qx is px:
                copies[slot] = send(half.at[qx, qy], land.at[mx, my], send_sems.at[0, base + slot],
                                    recv_sems.at[0, base + slot], {"gx": qx, "gy": qy})
    result = half[mx, my]
    for slot, qx, qy in reversed(order):
        copies[slot].wait()
        result = result + land[qx, qy]
    total[mz, mx, my] = result
    own = total.at[mz, mx, my]
    for slot, qx, qy in order:
        copies[slot] = send(own, own, send_sems.at[1, base + slot], recv_sems.at[1, base + slot], {"gx": qx, "gy": qy})
    across = []
    for i, px in reversed(list(enumerate(groups))):
        for slot, qx, qy in order:
            if qx is px:
                copies[slot].wait()
        block = total.at[mz, px]
        for d, p in enumerate(cores):
            across.append(send(block, block, send_sems.at[1, i * (nz - 1) + d], recv_sems.at[1, i * (nz - 1) + d], {"gz": p}))
    for copy in across:
        copy.wait()


def stages_kernel(axes, sizes, cells, x_ref, start_ref, factor_ref, rows_ref, gram_ref, *scratch):
    nz, ny, nx = sizes
    targets = flat_targets(nx, ny, nz)
    gram, field, fibres, packed, load_sems, send_first, recv_first = scratch[:7]
    packed_second, land, send_second, recv_second, start, start_sem = scratch[7:13]
    half = (len(scratch) - 13) // 2
    reduces = scratch[13 : 13 + half], scratch[13 + half :]
    start_load = pltpu.make_async_copy(start_ref, start, start_sem)

    def reduced(reduce_scratch, into):
        held, total = reduce_scratch[0], reduce_scratch[4]
        held[...] = gram[...].reshape(held.shape)
        flat_reduce(nx, ny, nz, held, reduce_scratch[1:])
        into[...] = total[...].reshape(into.shape)

    first_exchange(nx, targets, x_ref, start_load, field, fibres, gram, packed, load_sems, send_first, recv_first)
    reduced(reduces[0], gram)
    factor = power_steps(gram, start[...])
    factor_ref[...] = factor
    second_exchange(ny, cells, factor, fibres, rows_ref, gram, packed_second, land, send_second, recv_second)
    reduced(reduces[1], gram_ref)


def stages(field, start, axes, sizes, cells):
    nz, ny, nx = sizes
    depth, rows, columns = field.shape
    rank, extent = start.shape
    width = columns // nx
    ranks = rank // ny
    gram_shape = (len(upper_blocks(extent // LANES)) * LANES, LANES)
    blocked, reduce_scratch = flat_plan(gram_shape[0], nx, ny, nz)
    reduce_scratch = [pltpu.VMEM(blocked, jnp.float32)] + reduce_scratch
    first, second = depth * (nx - 1), depth * (ny - 1)
    return pl.pallas_call(
        functools.partial(stages_kernel, axes, sizes, cells),
        out_shape=(
            jax.ShapeDtypeStruct((rank, extent), jnp.float32),
            jax.ShapeDtypeStruct((ny, depth, ranks, width), jnp.float32),
            jax.ShapeDtypeStruct(gram_shape, jnp.float32),
        ),
        in_specs=[pl.BlockSpec(memory_space=pltpu.HBM)] * 2,
        out_specs=(VMEM, VMEM, VMEM),
        scratch_shapes=[
            pltpu.VMEM(gram_shape, jnp.float32),
            pltpu.VMEM((depth, rows, columns), jnp.float32),
            pltpu.VMEM((depth, nx, rows, width), jnp.float32),
            pltpu.VMEM((depth, nx, rows, width), jnp.float32),
            pltpu.SemaphoreType.DMA((depth,)),
            pltpu.SemaphoreType.DMA((first,)),
            pltpu.SemaphoreType.DMA((first,)),
            pltpu.VMEM((depth, ny, ranks, width), jnp.float32),
            pltpu.VMEM((ny, depth, ranks, width), jnp.float32),
            pltpu.SemaphoreType.DMA((second,)),
            pltpu.SemaphoreType.DMA((second,)),
            pltpu.VMEM((rank, extent), jnp.float32),
            pltpu.SemaphoreType.DMA,
            *reduce_scratch,
            *reduce_scratch,
        ],
        compiler_params=pltpu.CompilerParams(collective_id=0, has_side_effects=True, vmem_limit_bytes=GRANT),
    )(field, start)


def in_hbm(x):
    return pltpu.with_memory_space_constraint(x, pltpu.HBM)


def local(nx, ny, nz, species_field, start_first, start_second):
    depth, rows, columns = species_field.shape
    rank, extent = start_first.shape[1], start_second.shape[0]
    species, ranks = S // nx, rank // ny
    cells = LANES // species
    fits = (
        columns % (nx * LANES) == 0
        and columns // nx == extent
        and nx * rows == extent
        and species == ny
        and extent % LANES == 0
        and nx * rows % LANES == 0
        and ranks % 8 == 0
        and len(upper_blocks(extent // LANES)) * LANES % (8 * nx * ny * nz) == 0
    )
    if not fits:
        return local_general(nx, ny, nz, species_field, start_first, start_second)
    axes, sizes = ("gz", "gy", "gx"), (nz, ny, nx)
    factor_first, rows_second, gram_second = stages(in_hbm(species_field), in_hbm(start_first.T), axes, sizes, cells)
    rows_second = rows_second.reshape(species * depth * ranks, extent)
    factor_first, factor_second, core = pl.pallas_call(
        second_power_kernel,
        out_shape=(
            jax.ShapeDtypeStruct((rank, extent), jnp.float32),
            jax.ShapeDtypeStruct((rank, extent), jnp.float32),
            jax.ShapeDtypeStruct((rows_second.shape[0], rank), jnp.float32),
        ),
        in_specs=[VMEM, VMEM, VMEM, VMEM],
        out_specs=(VMEM, VMEM, VMEM),
        compiler_params=pltpu.CompilerParams(vmem_limit_bytes=GRANT),
    )(gram_second, start_second.T, rows_second, factor_first)
    return (factor_first.T, factor_second.T, core.reshape(species, depth, ranks, rank))


def solution(mesh):
    return jax.shard_map(
        functools.partial(local, mesh.shape["gx"], mesh.shape["gy"], mesh.shape["gz"]),
        mesh=mesh,
        in_specs=(P("gz", "gx", "gy"), P(), P()),
        out_specs=(P(), P(), P("gx", "gz", "gy", None)),
        check_vma=False,
    )
```

```python
import functools

import jax
import jax.numpy as jnp
from jax import lax
from jax.experimental import pallas as pl
from jax.experimental.pallas import tpu as pltpu
from jax.sharding import PartitionSpec as P

S = 16
ITERS = 2
LANES = 128
GRANT = 32 * 2**20
MESH = pl.DeviceIdType.MESH
VMEM = pl.BlockSpec(memory_space=pltpu.VMEM)

exact_precision = lax.Precision.HIGHEST


def dot_dims(a, b, contract_a, contract_b):
    return lax.dot_general(
        a, b, (((contract_a,), (contract_b,)), ((), ())),
        precision=exact_precision, preferred_element_type=jnp.float32,
    )


def partners(n, me):
    if n == 4:
        return [3 - me, lax.rem(me + 2, 4), me + 1 - 2 * lax.rem(me, 2)]
    return [lax.rem(me + d, n) for d in range(1, n)]


def send(src, dst, send_sem, recv_sem, target):
    copy = pltpu.make_async_remote_copy(
        src_ref=src, dst_ref=dst, send_sem=send_sem, recv_sem=recv_sem,
        device_id=target, device_id_type=MESH,
    )
    copy.start()
    return copy


def say_hello(targets):
    barrier = pltpu.get_barrier_semaphore()
    for target in targets:
        pl.semaphore_signal(barrier, inc=1, device_id=target, device_id_type=MESH)


def hear_hello(targets):
    pl.semaphore_wait(pltpu.get_barrier_semaphore(), len(targets))


def greet(targets):
    say_hello(targets)
    hear_hello(targets)


def axis_peers(axes, sizes):
    return [{axis: p} for axis, n in zip(axes, sizes) for p in partners(n, lax.axis_index(axis))]


def reduce_blocks(axes, sizes, splits, x_ref, o_ref, scratch):
    levels = len(axes)
    landing, totals = scratch[:levels], scratch[levels : 2 * levels - 1]
    send_sems, recv_sems = scratch[2 * levels - 1 :]
    me = [lax.axis_index(axis) for axis in axes]
    peers = [partners(n, m) for n, m in zip(sizes, me)]
    spot = [m if split > 1 else 0 for m, split in zip(me, splits)]
    sem = 0
    held = x_ref
    for level in range(levels):
        axis, n, split = axes[level], sizes[level], splits[level]
        land = landing[level]
        copies = []
        for p in peers[level]:
            src = held.at[p] if split > 1 else held.at[0]
            copies.append(send(src, land.at[me[level]], send_sems.at[sem], recv_sems.at[sem], {axis: p}))
            sem += 1
        land[me[level]] = held[spot[level]]
        for copy in copies:
            copy.wait()
        total = land[0]
        for source in range(1, n):
            total = total + land[source]
        if level < levels - 1:
            totals[level][...] = total
            held = totals[level]
        else:
            o_ref[tuple(spot)] = total

    for level in reversed(range(levels)):
        if splits[level] == 1:
            continue
        block = o_ref.at[tuple(spot[: level + 1])]
        copies = []
        for p in peers[level]:
            copies.append(send(block, block, send_sems.at[sem], recv_sems.at[sem], {axes[level]: p}))
            sem += 1
        for copy in copies:
            copy.wait()


def all_reduce_kernel(axes, sizes, splits, x_ref, o_ref, *scratch):
    greet(axis_peers(axes, sizes))
    reduce_blocks(axes, sizes, splits, x_ref, o_ref, scratch)


def reduce_plan(rows, columns, sizes):
    splits = []
    for n in sizes:
        splits.append(n if rows % n == 0 else 1)
        rows //= splits[-1]
    scratch = [
        pltpu.VMEM((n, *splits[level + 1 :], rows, columns), jnp.float32)
        for level, n in enumerate(sizes)
    ]
    scratch += [pltpu.VMEM((*splits[level + 1 :], rows, columns), jnp.float32) for level in range(len(sizes) - 1)]
    count = sum(n - 1 for n in sizes) + sum(n - 1 for n, split in zip(sizes, splits) if split > 1)
    scratch += [pltpu.SemaphoreType.DMA((count,)), pltpu.SemaphoreType.DMA((count,))]
    return splits, (*splits, rows, columns), scratch


def all_reduce(x, axes, sizes, collective_id):
    splits, blocked, scratch = reduce_plan(*x.shape, sizes)
    out = pl.pallas_call(
        functools.partial(all_reduce_kernel, axes, sizes, splits),
        out_shape=jax.ShapeDtypeStruct(blocked, jnp.float32),
        in_specs=[VMEM],
        out_specs=VMEM,
        scratch_shapes=scratch,
        compiler_params=pltpu.CompilerParams(collective_id=collective_id, has_side_effects=True),
    )(x.reshape(blocked))
    return out.reshape(x.shape)


def fibres_kernel(n, x_ref, o_ref, send_sems, recv_sems):
    me = lax.axis_index("gx")
    depth, rows, width = x_ref.shape[0], x_ref.shape[1], o_ref.shape[-1]
    peers = partners(n, me)
    greet([{"gx": p} for p in peers])
    copies = []
    for turn, p in enumerate(peers):
        columns = pl.ds(pl.multiple_of(p * width, width), width)
        copies.append(
            send(x_ref.at[:, :, columns], o_ref.at[:, me], send_sems.at[turn], recv_sems.at[turn], {"gx": p})
        )
    own = pl.ds(pl.multiple_of(me * width, width), width)
    for level in range(depth):
        o_ref[level, me] = x_ref[level, :, own]
    for copy in copies:
        copy.wait()


def gather_fibres(field, n):
    depth, rows, columns = field.shape
    width = columns // n
    if width % 128:
        return lax.all_to_all(field, "gx", split_axis=2, concat_axis=1, tiled=True)
    out = pl.pallas_call(
        functools.partial(fibres_kernel, n),
        out_shape=jax.ShapeDtypeStruct((depth, n, rows, width), jnp.float32),
        in_specs=[VMEM],
        out_specs=VMEM,
        scratch_shapes=[pltpu.SemaphoreType.DMA((n - 1,)), pltpu.SemaphoreType.DMA((n - 1,))],
        compiler_params=pltpu.CompilerParams(collective_id=0, has_side_effects=True),
    )(field)
    return out.reshape(depth, n * rows, width)


def exchange_kernel(nx, ny, x_ref, o_ref, send_sems, recv_sems):
    mx, my = lax.axis_index("gx"), lax.axis_index("gy")
    peers = [(px, my) for px in partners(nx, mx)]
    for py in partners(ny, my):
        peers += [(px, py) for px in partners(nx, mx) + [mx]]
    greet([{"gx": px, "gy": py} for px, py in peers])
    copies = []
    for turn, (px, py) in enumerate(peers):
        copies.append(
            send(x_ref.at[py, px], o_ref.at[my, mx], send_sems.at[turn], recv_sems.at[turn], {"gx": px, "gy": py})
        )
    o_ref[my, mx] = x_ref[my, mx]
    for copy in copies:
        copy.wait()


def exchange(blocks):
    ny, nx = blocks.shape[:2]
    count = nx * ny - 1
    return pl.pallas_call(
        functools.partial(exchange_kernel, nx, ny),
        out_shape=jax.ShapeDtypeStruct(blocks.shape, jnp.float32),
        in_specs=[VMEM],
        out_specs=VMEM,
        scratch_shapes=[pltpu.SemaphoreType.DMA((count,)), pltpu.SemaphoreType.DMA((count,))],
        compiler_params=pltpu.CompilerParams(collective_id=1, has_side_effects=True),
    )(blocks)


def inverse_lower(cross):
    rank = cross.shape[0]
    groups = rank // 8
    local_row = lax.broadcasted_iota(jnp.int32, (8, rank), 0)
    lane = lax.broadcasted_iota(jnp.int32, (8, rank), 1)

    def row_of(block, r):
        return jnp.broadcast_to(block[r : r + 1], (8, rank))

    def column_of(block, c):
        return jnp.broadcast_to(block[:, c : c + 1], (8, rank))

    rest = [cross[8 * g : 8 * g + 8] for g in range(groups)]
    pivots = [column_of(rest[0], j) for j in range(8)]
    near = [column_of(rest[1], j) for j in range(8)] if groups > 1 else None
    done = []
    for k in range(groups):
        low = 8 * k
        next_pivots = [column_of(rest[k + 1], low + 8 + j) for j in range(8)] if k + 1 < groups else None
        next_near = [column_of(rest[k + 2], low + 8 + j) for j in range(8)] if k + 2 < groups else None
        columns = {(j, k + 1): near[j] for j in range(8)} if k + 1 < groups else {}
        for g in range(k + 2, groups):
            for j in range(8):
                columns[j, g] = column_of(rest[g], low + j)
        own_lanes = (lane >= low) & (lane < low + 8)
        rest[k] = jnp.where(own_lanes, jnp.where(lane == local_row + low, 1.0, 0.0), rest[k])
        for g in range(k + 1, groups):
            rest[g] = jnp.where(own_lanes, 0.0, rest[g])
        diagonal = jnp.ones((8, rank), jnp.float32)
        factors = []
        for j in range(8):
            pivot = row_of(pivots[j], j)
            diagonal = jnp.where(local_row == j, pivot, diagonal)
            reciprocal = 1.0 / pivot
            factor = pivots[j] * reciprocal
            factors.append(factor)
            values = {other: row_of(pivots[j], other) for other in range(j + 1, 8)}
            for other in range(j + 1, 8):
                if other == j + 1:
                    change = (pivots[j] * values[other]) * reciprocal
                else:
                    change = factor * values[other]
                pivots[other] = pivots[other] - change
            own_row = row_of(rest[k], j)
            rest[k] = rest[k] - jnp.where(local_row > j, factor, 0.0) * own_row
            if k + 1 < groups:
                ahead = [row_of(columns[j, k + 1], other) for other in range(8)]
            for g in range(k + 1, min(k + 3, groups)):
                factor = columns[j, g] * reciprocal
                for other in range(j + 1, 8):
                    columns[other, g] = columns[other, g] - factor * values[other]
                following = next_pivots if g == k + 1 else next_near
                for other in range(8):
                    following[other] = following[other] - factor * ahead[other]
                rest[g] = rest[g] - factor * own_row
        done.append(jnp.where(lane < low + 8, rest[k] * (1.0 / jnp.sqrt(diagonal)), 0.0))
        if k + 3 < groups:
            solved = rest[k] * (1.0 / diagonal)
            for j in range(7, 0, -1):
                above = jnp.zeros((8, rank), jnp.float32)
                for i in range(j):
                    above = jnp.where(local_row == i, row_of(factors[i], j), above)
                solved = solved - above * row_of(solved, j)
            for j in range(8):
                own_row = row_of(solved, j)
                for g in range(k + 3, groups):
                    rest[g] = rest[g] - columns[j, g] * own_row
        pivots, near = next_pivots, next_near
    return jnp.concatenate(done, axis=0)


def power_general_kernel(gram_ref, start_ref, out_ref):
    current = start_ref[...]
    for turn in range(ITERS):
        images = dot_dims(gram_ref[...], current, 1, 0)
        cross = dot_dims(images, images, 0, 0)
        current = dot_dims(images, inverse_lower(cross), 1, 1)
    out_ref[...] = current


def leading(gram, start):
    return pl.pallas_call(
        power_general_kernel,
        out_shape=jax.ShapeDtypeStruct(start.shape, jnp.float32),
        in_specs=[VMEM, VMEM],
        out_specs=VMEM,
    )(gram, start)


def local_general(nx, ny, nz, species_field, start_first, start_second):
    axes, sizes = ("gz", "gy", "gx"), (nz, ny, nx)
    fibres = gather_fibres(species_field, nx)
    partial_gram = jnp.einsum("zic,zjc->ij", fibres, fibres, precision=exact_precision)
    gram_first = all_reduce(partial_gram, axes, sizes, 2)
    factor_first = leading(gram_first, start_first)

    depth = fibres.shape[0]
    cells = fibres.shape[2] // S
    rank = start_first.shape[1]
    species, ranks = S // nx, rank // ny
    projected = jnp.einsum("zim,ir->zmr", fibres, factor_first, precision=exact_precision)
    blocks = projected.reshape(depth, cells, nx, species, ny, ranks)
    blocks = blocks.transpose(4, 2, 1, 3, 0, 5).reshape(ny, nx, cells, species * depth * ranks)
    columns = exchange(blocks)
    columns = columns.reshape(ny * nx * cells, species * depth * ranks)
    partial_second = dot_dims(columns, columns, 1, 1)
    gram_second = all_reduce(partial_second, axes, sizes, 3)
    factor_second = leading(gram_second, start_second)
    core = dot_dims(columns, factor_second, 0, 0)
    core = core.reshape(species, depth, ranks, factor_second.shape[1])
    return (factor_first, factor_second, core)


def upper_blocks(count):
    return [(a, b) for a in range(count) for b in range(a, count)]


def add_gram(gram_ref, parts, contract, first):
    for slot, (a, b) in enumerate(upper_blocks(len(parts))):
        block = pl.ds(slot * LANES, LANES)
        term = dot_dims(parts[a], parts[b], contract, contract)
        gram_ref[block, :] = term if first else gram_ref[block, :] + term


def parts_of(x):
    high = x.astype(jnp.bfloat16)
    left = x - high.astype(jnp.float32)
    middle = left.astype(jnp.bfloat16)
    return high, middle, (left - middle.astype(jnp.float32)).astype(jnp.bfloat16)


def dot_parts(a, b, contract_a, contract_b):
    rows = a[0].shape[0]

    def dot(x, y):
        return lax.dot_general(
            x, y, (((contract_a,), (contract_b,)), ((), ())), preferred_element_type=jnp.float32
        )

    by_high = dot(jnp.concatenate(a, axis=0), b[0])
    by_middle = dot(jnp.concatenate(a[:2], axis=0), b[1])
    small = by_high[2 * rows :] + by_middle[rows:] + dot(a[0], b[2])
    return (small + (by_high[rows : 2 * rows] + by_middle[:rows])) + by_high[:rows]


def whole_gram(gram):
    count = 1
    while count * (count + 1) // 2 * LANES < gram.shape[0]:
        count += 1
    block = {}
    for slot, (a, b) in enumerate(upper_blocks(count)):
        block[a, b] = gram[slot * LANES : (slot + 1) * LANES, :]
        if a != b:
            block[b, a] = block[a, b].T
    return jnp.concatenate(
        [jnp.concatenate([block[a, b] for b in range(count)], axis=1) for a in range(count)], axis=0
    )


def power_steps(gram_ref, current):
    gram = parts_of(whole_gram(gram_ref[...]))
    for turn in range(ITERS):
        images = parts_of(dot_parts(parts_of(current), gram, 1, 0))
        cross = dot_parts(images, images, 1, 1)
        current = dot_parts(parts_of(inverse_lower(cross)), images, 1, 0)
    return current


def second_power_kernel(gram_ref, start_ref, rows_ref, first_ref, first_out_ref, out_ref, core_ref):
    first_out_ref[...] = first_ref[...]
    current = power_steps(gram_ref, start_ref[...])
    out_ref[...] = current
    core_ref[...] = dot_dims(rows_ref[...], current, 1, 1)


def species_major(block, order):
    high = block.astype(jnp.bfloat16)
    left = block - high.astype(jnp.float32)
    middle = left.astype(jnp.bfloat16)
    low = (left - middle.astype(jnp.float32)).astype(jnp.bfloat16)
    moved = [
        lax.dot_general(part, order, (((1,), (0,)), ((), ())), preferred_element_type=jnp.float32)
        for part in (high, middle, low)
    ]
    return (moved[0] + moved[1]) + moved[2]


def first_exchange(n, targets, x_ref, start_load, field, fibres, gram, packed, load_sems, send_sems, recv_sems):
    me = lax.axis_index("gx")
    depth, rows, columns = field.shape
    span = n * LANES
    cells = span // S
    width = columns // n
    loads = [pltpu.make_async_copy(x_ref.at[z], field.at[z], load_sems.at[z]) for z in range(depth)]
    for load in loads + [start_load]:
        load.start()
    say_hello(targets)
    peers = partners(n, me)
    source = lax.broadcasted_iota(jnp.int32, (span, span), 0)
    target = lax.broadcasted_iota(jnp.int32, (span, span), 1)
    species = lax.shift_right_logical(target, cells.bit_length() - 1)
    order = jnp.where(source == (target & (cells - 1)) * S + species, 1.0, 0.0).astype(jnp.bfloat16)
    copies = []
    for level in range(depth):
        loads[level].wait()
        for chunk in range(columns // span):
            moved = species_major(field[level, :, chunk * span : (chunk + 1) * span], order)
            lanes = pl.ds(chunk * LANES, LANES)
            for p in range(n):
                packed[level, p, :, lanes] = moved[:, p * LANES : (p + 1) * LANES]
        if level == 0:
            hear_hello(targets)
        turns = list(enumerate(peers))
        if level > 0:
            turns = turns[-1:] + turns[:-1]
        for turn, p in turns:
            sem = level * (n - 1) + turn
            copies.append(
                send(packed.at[level, p], fibres.at[level, me], send_sems.at[sem], recv_sems.at[sem], {"gx": p})
            )
        fibres[level, me] = packed[level, me]
    for level in range(depth):
        for copy in copies[level * (n - 1) : (level + 1) * (n - 1)]:
            copy.wait()
        whole = fibres[level].reshape(n * rows, width)
        parts = [whole[a : a + LANES] for a in range(0, n * rows, LANES)]
        add_gram(gram, parts, 1, level == 0)
    start_load.wait()


def second_exchange(n, cells, factor, fibres, rows_ref, gram, packed, land, send_sems, recv_sems):
    me = lax.axis_index("gy")
    depth, ranks, width = packed.shape[0], packed.shape[2], packed.shape[3]
    peers = partners(n, me)
    copies = []
    for level in range(depth):
        whole = fibres[level].reshape(factor.shape[1], width)
        packed[level] = dot_dims(factor, whole, 1, 0).reshape(n, ranks, width)
        for turn, p in enumerate(peers):
            sem = level * (n - 1) + turn
            copies.append(
                send(packed.at[level, p], land.at[me, level], send_sems.at[sem], recv_sems.at[sem], {"gy": p})
            )
        land[me, level] = packed[level, me]
    lane_group = lax.shift_right_logical(
        lax.broadcasted_iota(jnp.int32, (ranks, LANES), 1), cells.bit_length() - 1
    )
    for level in range(depth):
        for copy in copies[level * (n - 1) : (level + 1) * (n - 1)]:
            copy.wait()
        chunks = width // LANES
        for tile in range(chunks):
            for s in range(n):
                merged = None
                for g in range(n):
                    t, chunk = divmod(n * tile + g, chunks)
                    turned = land[t, level, :, chunk * LANES : (chunk + 1) * LANES]
                    if g != s:
                        turned = pltpu.roll(turned, cells * ((g - s) % n), 1)
                    merged = turned if g == 0 else jnp.where(lane_group == g, turned, merged)
                rows_ref[s, level, :, tile * LANES : (tile + 1) * LANES] = merged
        whole = rows_ref[:, level].reshape(n * ranks, width)
        parts = [whole[:, a : a + LANES] for a in range(0, width, LANES)]
        add_gram(gram, parts, 0, level == 0)


def flat_plan(rows, nx, ny, nz):
    piece = rows // (nx * ny * nz)
    count = nx * (nz - 1) + nx * ny - 1
    return (nz, nx, ny, piece, LANES), [
        pltpu.VMEM((nz - 1, nx, ny, piece, LANES), jnp.float32),
        pltpu.VMEM((nx, ny, piece, LANES), jnp.float32),
        pltpu.VMEM((nx, ny, piece, LANES), jnp.float32),
        pltpu.VMEM((nz, nx, ny, piece, LANES), jnp.float32),
        pltpu.SemaphoreType.DMA((2, count)),
        pltpu.SemaphoreType.DMA((2, count)),
    ]


def flat_reduce(nx, ny, nz, held, scratch):
    land_core, half, land, total, send_sems, recv_sems = scratch
    mx, my, mz = lax.axis_index("gx"), lax.axis_index("gy"), lax.axis_index("gz")
    cores, columns, planes = partners(nz, mz), partners(nx, mx), partners(ny, my)
    groups = columns + [mx]
    base = nx * (nz - 1)

    def turns(px):
        return [(px, py) for py in planes + ([] if px is mx else [my])]

    order = [(i, px, py) for i, (px, py) in enumerate(sum((turns(px) for px in groups), []))]

    across = []
    for i, px in enumerate(groups):
        across.append([
            send(held.at[p, px], land_core.at[d, px], send_sems.at[0, i * (nz - 1) + d],
                 recv_sems.at[0, i * (nz - 1) + d], {"gz": p})
            for d, p in enumerate(cores)
        ])
    copies = {}
    for i, px in enumerate(groups):
        for copy in across[i]:
            copy.wait()
        summed = held[mz, px]
        for d in range(nz - 1):
            summed = summed + land_core[d, px]
        half[px] = summed
        for slot, qx, qy in order:
            if qx is px:
                copies[slot] = send(half.at[qx, qy], land.at[mx, my], send_sems.at[0, base + slot],
                                    recv_sems.at[0, base + slot], {"gx": qx, "gy": qy})
    result = half[mx, my]
    for slot, qx, qy in reversed(order):
        copies[slot].wait()
        result = result + land[qx, qy]
    total[mz, mx, my] = result
    own = total.at[mz, mx, my]
    for slot, qx, qy in order:
        copies[slot] = send(own, own, send_sems.at[1, base + slot], recv_sems.at[1, base + slot], {"gx": qx, "gy": qy})
    across = []
    for i, px in reversed(list(enumerate(groups))):
        for slot, qx, qy in order:
            if qx is px:
                copies[slot].wait()
        block = total.at[mz, px]
        for d, p in enumerate(cores):
            across.append(send(block, block, send_sems.at[1, i * (nz - 1) + d], recv_sems.at[1, i * (nz - 1) + d], {"gz": p}))
    for copy in across:
        copy.wait()


def stages_kernel(axes, sizes, cells, x_ref, start_ref, factor_ref, rows_ref, gram_ref, *scratch):
    nz, ny, nx = sizes
    targets = axis_peers(axes, sizes)
    gram, field, fibres, packed, load_sems, send_first, recv_first = scratch[:7]
    packed_second, land, send_second, recv_second, start, start_sem = scratch[7:13]
    half = (len(scratch) - 13) // 2
    reduces = scratch[13 : 13 + half], scratch[13 + half :]
    start_load = pltpu.make_async_copy(start_ref, start, start_sem)

    def reduced(reduce_scratch, into):
        held, total = reduce_scratch[0], reduce_scratch[4]
        held[...] = gram[...].reshape(held.shape)
        flat_reduce(nx, ny, nz, held, reduce_scratch[1:])
        into[...] = total[...].reshape(into.shape)

    first_exchange(nx, targets, x_ref, start_load, field, fibres, gram, packed, load_sems, send_first, recv_first)
    reduced(reduces[0], gram)
    factor = power_steps(gram, start[...])
    factor_ref[...] = factor
    second_exchange(ny, cells, factor, fibres, rows_ref, gram, packed_second, land, send_second, recv_second)
    reduced(reduces[1], gram_ref)


def stages(field, start, axes, sizes, cells):
    nz, ny, nx = sizes
    depth, rows, columns = field.shape
    rank, extent = start.shape
    width = columns // nx
    ranks = rank // ny
    gram_shape = (len(upper_blocks(extent // LANES)) * LANES, LANES)
    blocked, reduce_scratch = flat_plan(gram_shape[0], nx, ny, nz)
    reduce_scratch = [pltpu.VMEM(blocked, jnp.float32)] + reduce_scratch
    first, second = depth * (nx - 1), depth * (ny - 1)
    return pl.pallas_call(
        functools.partial(stages_kernel, axes, sizes, cells),
        out_shape=(
            jax.ShapeDtypeStruct((rank, extent), jnp.float32),
            jax.ShapeDtypeStruct((ny, depth, ranks, width), jnp.float32),
            jax.ShapeDtypeStruct(gram_shape, jnp.float32),
        ),
        in_specs=[pl.BlockSpec(memory_space=pltpu.HBM)] * 2,
        out_specs=(VMEM, VMEM, VMEM),
        scratch_shapes=[
            pltpu.VMEM(gram_shape, jnp.float32),
            pltpu.VMEM((depth, rows, columns), jnp.float32),
            pltpu.VMEM((depth, nx, rows, width), jnp.float32),
            pltpu.VMEM((depth, nx, rows, width), jnp.float32),
            pltpu.SemaphoreType.DMA((depth,)),
            pltpu.SemaphoreType.DMA((first,)),
            pltpu.SemaphoreType.DMA((first,)),
            pltpu.VMEM((depth, ny, ranks, width), jnp.float32),
            pltpu.VMEM((ny, depth, ranks, width), jnp.float32),
            pltpu.SemaphoreType.DMA((second,)),
            pltpu.SemaphoreType.DMA((second,)),
            pltpu.VMEM((rank, extent), jnp.float32),
            pltpu.SemaphoreType.DMA,
            *reduce_scratch,
            *reduce_scratch,
        ],
        compiler_params=pltpu.CompilerParams(collective_id=0, has_side_effects=True, vmem_limit_bytes=GRANT),
    )(field, start)


def in_hbm(x):
    return pltpu.with_memory_space_constraint(x, pltpu.HBM)


def local(nx, ny, nz, species_field, start_first, start_second):
    depth, rows, columns = species_field.shape
    rank, extent = start_first.shape[1], start_second.shape[0]
    species, ranks = S // nx, rank // ny
    cells = LANES // species
    fits = (
        columns % (nx * LANES) == 0
        and columns // nx == extent
        and nx * rows == extent
        and species == ny
        and extent % LANES == 0
        and nx * rows % LANES == 0
        and ranks % 8 == 0
        and len(upper_blocks(extent // LANES)) * LANES % (8 * nx * ny * nz) == 0
    )
    if not fits:
        return local_general(nx, ny, nz, species_field, start_first, start_second)
    axes, sizes = ("gz", "gy", "gx"), (nz, ny, nx)
    factor_first, rows_second, gram_second = stages(in_hbm(species_field), in_hbm(start_first.T), axes, sizes, cells)
    rows_second = rows_second.reshape(species * depth * ranks, extent)
    factor_first, factor_second, core = pl.pallas_call(
        second_power_kernel,
        out_shape=(
            jax.ShapeDtypeStruct((rank, extent), jnp.float32),
            jax.ShapeDtypeStruct((rank, extent), jnp.float32),
            jax.ShapeDtypeStruct((rows_second.shape[0], rank), jnp.float32),
        ),
        in_specs=[VMEM, VMEM, VMEM, VMEM],
        out_specs=(VMEM, VMEM, VMEM),
        compiler_params=pltpu.CompilerParams(vmem_limit_bytes=GRANT),
    )(gram_second, start_second.T, rows_second, factor_first)
    return (factor_first.T, factor_second.T, core.reshape(species, depth, ranks, rank))


def solution(mesh):
    return jax.shard_map(
        functools.partial(local, mesh.shape["gx"], mesh.shape["gy"], mesh.shape["gz"]),
        mesh=mesh,
        in_specs=(P("gz", "gx", "gy"), P(), P()),
        out_specs=(P(), P(), P("gx", "gz", "gy", None)),
        check_vma=False,
    )
```

```python
import functools

import jax
import jax.numpy as jnp
from jax import lax
from jax.experimental import pallas as pl
from jax.experimental.pallas import tpu as pltpu
from jax.sharding import PartitionSpec as P

S = 16
ITERS = 2
LANES = 128
GRANT = 32 * 2**20
MESH = pl.DeviceIdType.MESH
VMEM = pl.BlockSpec(memory_space=pltpu.VMEM)

exact_precision = lax.Precision.HIGHEST


def dot_dims(a, b, contract_a, contract_b):
    return lax.dot_general(
        a, b, (((contract_a,), (contract_b,)), ((), ())),
        precision=exact_precision, preferred_element_type=jnp.float32,
    )


def partners(n, me):
    if n == 4:
        return [3 - me, lax.rem(me + 2, 4), me + 1 - 2 * lax.rem(me, 2)]
    return [lax.rem(me + d, n) for d in range(1, n)]


def far_partners(n, me):
    if n == 4:
        return [lax.rem(me + 2, 4), 3 - me, me + 1 - 2 * lax.rem(me, 2)]
    return partners(n, me)


def send(src, dst, send_sem, recv_sem, target):
    copy = pltpu.make_async_remote_copy(
        src_ref=src, dst_ref=dst, send_sem=send_sem, recv_sem=recv_sem,
        device_id=target, device_id_type=MESH,
    )
    copy.start()
    return copy


def say_hello(targets):
    barrier = pltpu.get_barrier_semaphore()
    for target in targets:
        pl.semaphore_signal(barrier, inc=1, device_id=target, device_id_type=MESH)


def hear_hello(targets):
    pl.semaphore_wait(pltpu.get_barrier_semaphore(), len(targets))


def greet(targets):
    say_hello(targets)
    hear_hello(targets)


def axis_peers(axes, sizes):
    return [{axis: p} for axis, n in zip(axes, sizes) for p in partners(n, lax.axis_index(axis))]


def reduce_blocks(axes, sizes, splits, x_ref, o_ref, scratch):
    levels = len(axes)
    landing, totals = scratch[:levels], scratch[levels : 2 * levels - 1]
    send_sems, recv_sems = scratch[2 * levels - 1 :]
    me = [lax.axis_index(axis) for axis in axes]
    peers = [partners(n, m) for n, m in zip(sizes, me)]
    spot = [m if split > 1 else 0 for m, split in zip(me, splits)]
    sem = 0
    held = x_ref
    for level in range(levels):
        axis, n, split = axes[level], sizes[level], splits[level]
        land = landing[level]
        copies = []
        for p in peers[level]:
            src = held.at[p] if split > 1 else held.at[0]
            copies.append(send(src, land.at[me[level]], send_sems.at[sem], recv_sems.at[sem], {axis: p}))
            sem += 1
        land[me[level]] = held[spot[level]]
        for copy in copies:
            copy.wait()
        total = land[0]
        for source in range(1, n):
            total = total + land[source]
        if level < levels - 1:
            totals[level][...] = total
            held = totals[level]
        else:
            o_ref[tuple(spot)] = total

    for level in reversed(range(levels)):
        if splits[level] == 1:
            continue
        block = o_ref.at[tuple(spot[: level + 1])]
        copies = []
        for p in peers[level]:
            copies.append(send(block, block, send_sems.at[sem], recv_sems.at[sem], {axes[level]: p}))
            sem += 1
        for copy in copies:
            copy.wait()


def all_reduce_kernel(axes, sizes, splits, x_ref, o_ref, *scratch):
    greet(axis_peers(axes, sizes))
    reduce_blocks(axes, sizes, splits, x_ref, o_ref, scratch)


def reduce_plan(rows, columns, sizes):
    splits = []
    for n in sizes:
        splits.append(n if rows % n == 0 else 1)
        rows //= splits[-1]
    scratch = [
        pltpu.VMEM((n, *splits[level + 1 :], rows, columns), jnp.float32)
        for level, n in enumerate(sizes)
    ]
    scratch += [pltpu.VMEM((*splits[level + 1 :], rows, columns), jnp.float32) for level in range(len(sizes) - 1)]
    count = sum(n - 1 for n in sizes) + sum(n - 1 for n, split in zip(sizes, splits) if split > 1)
    scratch += [pltpu.SemaphoreType.DMA((count,)), pltpu.SemaphoreType.DMA((count,))]
    return splits, (*splits, rows, columns), scratch


def all_reduce(x, axes, sizes, collective_id):
    splits, blocked, scratch = reduce_plan(*x.shape, sizes)
    out = pl.pallas_call(
        functools.partial(all_reduce_kernel, axes, sizes, splits),
        out_shape=jax.ShapeDtypeStruct(blocked, jnp.float32),
        in_specs=[VMEM],
        out_specs=VMEM,
        scratch_shapes=scratch,
        compiler_params=pltpu.CompilerParams(collective_id=collective_id, has_side_effects=True),
    )(x.reshape(blocked))
    return out.reshape(x.shape)


def fibres_kernel(n, x_ref, o_ref, send_sems, recv_sems):
    me = lax.axis_index("gx")
    depth, rows, width = x_ref.shape[0], x_ref.shape[1], o_ref.shape[-1]
    peers = partners(n, me)
    greet([{"gx": p} for p in peers])
    copies = []
    for turn, p in enumerate(peers):
        columns = pl.ds(pl.multiple_of(p * width, width), width)
        copies.append(
            send(x_ref.at[:, :, columns], o_ref.at[:, me], send_sems.at[turn], recv_sems.at[turn], {"gx": p})
        )
    own = pl.ds(pl.multiple_of(me * width, width), width)
    for level in range(depth):
        o_ref[level, me] = x_ref[level, :, own]
    for copy in copies:
        copy.wait()


def gather_fibres(field, n):
    depth, rows, columns = field.shape
    width = columns // n
    if width % 128:
        return lax.all_to_all(field, "gx", split_axis=2, concat_axis=1, tiled=True)
    out = pl.pallas_call(
        functools.partial(fibres_kernel, n),
        out_shape=jax.ShapeDtypeStruct((depth, n, rows, width), jnp.float32),
        in_specs=[VMEM],
        out_specs=VMEM,
        scratch_shapes=[pltpu.SemaphoreType.DMA((n - 1,)), pltpu.SemaphoreType.DMA((n - 1,))],
        compiler_params=pltpu.CompilerParams(collective_id=0, has_side_effects=True),
    )(field)
    return out.reshape(depth, n * rows, width)


def exchange_kernel(nx, ny, x_ref, o_ref, send_sems, recv_sems):
    mx, my = lax.axis_index("gx"), lax.axis_index("gy")
    peers = [(px, my) for px in partners(nx, mx)]
    for py in partners(ny, my):
        peers += [(px, py) for px in partners(nx, mx) + [mx]]
    greet([{"gx": px, "gy": py} for px, py in peers])
    copies = []
    for turn, (px, py) in enumerate(peers):
        copies.append(
            send(x_ref.at[py, px], o_ref.at[my, mx], send_sems.at[turn], recv_sems.at[turn], {"gx": px, "gy": py})
        )
    o_ref[my, mx] = x_ref[my, mx]
    for copy in copies:
        copy.wait()


def exchange(blocks):
    ny, nx = blocks.shape[:2]
    count = nx * ny - 1
    return pl.pallas_call(
        functools.partial(exchange_kernel, nx, ny),
        out_shape=jax.ShapeDtypeStruct(blocks.shape, jnp.float32),
        in_specs=[VMEM],
        out_specs=VMEM,
        scratch_shapes=[pltpu.SemaphoreType.DMA((count,)), pltpu.SemaphoreType.DMA((count,))],
        compiler_params=pltpu.CompilerParams(collective_id=1, has_side_effects=True),
    )(blocks)


def inverse_lower(cross):
    rank = cross.shape[0]
    groups = rank // 8
    local_row = lax.broadcasted_iota(jnp.int32, (8, rank), 0)
    lane = lax.broadcasted_iota(jnp.int32, (8, rank), 1)

    def row_of(block, r):
        return jnp.broadcast_to(block[r : r + 1], (8, rank))

    def column_of(block, c):
        return jnp.broadcast_to(block[:, c : c + 1], (8, rank))

    rest = [cross[8 * g : 8 * g + 8] for g in range(groups)]
    pivots = [column_of(rest[0], j) for j in range(8)]
    near = [column_of(rest[1], j) for j in range(8)] if groups > 1 else None
    done = []
    for k in range(groups):
        low = 8 * k
        next_pivots = [column_of(rest[k + 1], low + 8 + j) for j in range(8)] if k + 1 < groups else None
        next_near = [column_of(rest[k + 2], low + 8 + j) for j in range(8)] if k + 2 < groups else None
        columns = {(j, k + 1): near[j] for j in range(8)} if k + 1 < groups else {}
        for g in range(k + 2, groups):
            for j in range(8):
                columns[j, g] = column_of(rest[g], low + j)
        own_lanes = (lane >= low) & (lane < low + 8)
        rest[k] = jnp.where(own_lanes, jnp.where(lane == local_row + low, 1.0, 0.0), rest[k])
        for g in range(k + 1, groups):
            rest[g] = jnp.where(own_lanes, 0.0, rest[g])
        diagonal = jnp.ones((8, rank), jnp.float32)
        factors = []
        for j in range(8):
            pivot = row_of(pivots[j], j)
            diagonal = jnp.where(local_row == j, pivot, diagonal)
            reciprocal = 1.0 / pivot
            factor = pivots[j] * reciprocal
            factors.append(factor)
            values = {other: row_of(pivots[j], other) for other in range(j + 1, 8)}
            for other in range(j + 1, 8):
                if other == j + 1:
                    change = (pivots[j] * values[other]) * reciprocal
                else:
                    change = factor * values[other]
                pivots[other] = pivots[other] - change
            own_row = row_of(rest[k], j)
            rest[k] = rest[k] - jnp.where(local_row > j, factor, 0.0) * own_row
            if k + 1 < groups:
                ahead = [row_of(columns[j, k + 1], other) for other in range(8)]
            for g in range(k + 1, min(k + 3, groups)):
                factor = columns[j, g] * reciprocal
                for other in range(j + 1, 8):
                    columns[other, g] = columns[other, g] - factor * values[other]
                following = next_pivots if g == k + 1 else next_near
                for other in range(8):
                    following[other] = following[other] - factor * ahead[other]
                rest[g] = rest[g] - factor * own_row
        done.append(jnp.where(lane < low + 8, rest[k] * (1.0 / jnp.sqrt(diagonal)), 0.0))
        if k + 3 < groups:
            solved = rest[k] * (1.0 / diagonal)
            for j in range(7, 0, -1):
                above = jnp.zeros((8, rank), jnp.float32)
                for i in range(j):
                    above = jnp.where(local_row == i, row_of(factors[i], j), above)
                solved = solved - above * row_of(solved, j)
            for j in range(8):
                own_row = row_of(solved, j)
                for g in range(k + 3, groups):
                    rest[g] = rest[g] - columns[j, g] * own_row
        pivots, near = next_pivots, next_near
    return jnp.concatenate(done, axis=0)


def power_general_kernel(gram_ref, start_ref, out_ref):
    current = start_ref[...]
    for turn in range(ITERS):
        images = dot_dims(gram_ref[...], current, 1, 0)
        cross = dot_dims(images, images, 0, 0)
        current = dot_dims(images, inverse_lower(cross), 1, 1)
    out_ref[...] = current


def leading(gram, start):
    return pl.pallas_call(
        power_general_kernel,
        out_shape=jax.ShapeDtypeStruct(start.shape, jnp.float32),
        in_specs=[VMEM, VMEM],
        out_specs=VMEM,
    )(gram, start)


def local_general(nx, ny, nz, species_field, start_first, start_second):
    axes, sizes = ("gz", "gy", "gx"), (nz, ny, nx)
    fibres = gather_fibres(species_field, nx)
    partial_gram = jnp.einsum("zic,zjc->ij", fibres, fibres, precision=exact_precision)
    gram_first = all_reduce(partial_gram, axes, sizes, 2)
    factor_first = leading(gram_first, start_first)

    depth = fibres.shape[0]
    cells = fibres.shape[2] // S
    rank = start_first.shape[1]
    species, ranks = S // nx, rank // ny
    projected = jnp.einsum("zim,ir->zmr", fibres, factor_first, precision=exact_precision)
    blocks = projected.reshape(depth, cells, nx, species, ny, ranks)
    blocks = blocks.transpose(4, 2, 1, 3, 0, 5).reshape(ny, nx, cells, species * depth * ranks)
    columns = exchange(blocks)
    columns = columns.reshape(ny * nx * cells, species * depth * ranks)
    partial_second = dot_dims(columns, columns, 1, 1)
    gram_second = all_reduce(partial_second, axes, sizes, 3)
    factor_second = leading(gram_second, start_second)
    core = dot_dims(columns, factor_second, 0, 0)
    core = core.reshape(species, depth, ranks, factor_second.shape[1])
    return (factor_first, factor_second, core)


def upper_blocks(count):
    return [(a, b) for a in range(count) for b in range(a, count)]


def parts_of(x):
    high = x.astype(jnp.bfloat16)
    left = x - high.astype(jnp.float32)
    middle = left.astype(jnp.bfloat16)
    return high, middle, (left - middle.astype(jnp.float32)).astype(jnp.bfloat16)


def dot_parts(a, b, contract_a, contract_b):
    a, b = tuple(a), tuple(b)
    rows = a[0].shape[0]

    def dot(x, y):
        return lax.dot_general(
            x, y, (((contract_a,), (contract_b,)), ((), ())), preferred_element_type=jnp.float32
        )

    by_high = dot(jnp.concatenate(a, axis=0), b[0])
    by_middle = dot(jnp.concatenate(a[:2], axis=0), b[1])
    small = by_high[2 * rows :] + by_middle[rows:] + dot(a[0], b[2])
    return (small + (by_high[rows : 2 * rows] + by_middle[:rows])) + by_high[:rows]


def add_gram(gram_ref, parts, first):
    slot = 0
    for low in range(0, parts[0].shape[0], LANES):
        terms = dot_parts([x[low : low + LANES] for x in parts], [x[low:] for x in parts], 1, 1)
        for place in range(0, terms.shape[1], LANES):
            block = pl.ds(slot * LANES, LANES)
            term = terms[:, place : place + LANES]
            gram_ref[block, :] = term if first else gram_ref[block, :] + term
            slot += 1


def whole_gram(gram):
    count = 1
    while count * (count + 1) // 2 * LANES < gram.shape[0]:
        count += 1
    block = {}
    for slot, (a, b) in enumerate(upper_blocks(count)):
        block[a, b] = gram[slot * LANES : (slot + 1) * LANES, :]
        if a != b:
            block[b, a] = block[a, b].T
    return jnp.concatenate(
        [jnp.concatenate([block[a, b] for b in range(count)], axis=1) for a in range(count)], axis=0
    )


def power_steps(gram_ref, current):
    gram = parts_of(whole_gram(gram_ref[...]))
    for turn in range(ITERS):
        images = parts_of(dot_parts(parts_of(current), gram, 1, 0))
        cross = dot_parts(images, images, 1, 1)
        current = dot_parts(parts_of(inverse_lower(cross)), images, 1, 0)
    return current


def second_power_kernel(gram_ref, start_ref, rows_ref, first_ref, first_out_ref, out_ref, core_ref):
    first_out_ref[...] = first_ref[...]
    current = power_steps(gram_ref, start_ref[...])
    out_ref[...] = current
    core_ref[...] = dot_parts(parts_of(rows_ref[...]), parts_of(current), 1, 1)


def species_major(block, order):
    high = block.astype(jnp.bfloat16)
    left = block - high.astype(jnp.float32)
    middle = left.astype(jnp.bfloat16)
    low = (left - middle.astype(jnp.float32)).astype(jnp.bfloat16)
    moved = [
        lax.dot_general(part, order, (((1,), (0,)), ((), ())), preferred_element_type=jnp.float32)
        for part in (high, middle, low)
    ]
    return (moved[0] + moved[1]) + moved[2]


def first_exchange(n, targets, x_ref, start_load, field, fibres, split, gram, packed, load_sems, send_sems, recv_sems):
    me = lax.axis_index("gx")
    depth, rows, columns = field.shape
    span = n * LANES
    cells = span // S
    width = columns // n
    loads = [pltpu.make_async_copy(x_ref.at[z], field.at[z], load_sems.at[z]) for z in range(depth)]
    for load in loads + [start_load]:
        load.start()
    say_hello(targets)
    peers = far_partners(n, me)
    source = lax.broadcasted_iota(jnp.int32, (span, span), 0)
    target = lax.broadcasted_iota(jnp.int32, (span, span), 1)
    species = lax.shift_right_logical(target, cells.bit_length() - 1)
    order = jnp.where(source == (target & (cells - 1)) * S + species, 1.0, 0.0).astype(jnp.bfloat16)
    copies = []
    for level in range(depth):
        loads[level].wait()
        for chunk in range(columns // span):
            moved = species_major(field[level, :, chunk * span : (chunk + 1) * span], order)
            lanes = pl.ds(chunk * LANES, LANES)
            for p in range(n):
                packed[level, p, :, lanes] = moved[:, p * LANES : (p + 1) * LANES]
        if level == 0:
            hear_hello(targets)
        for turn, p in enumerate(peers):
            sem = level * (n - 1) + turn
            copies.append(
                send(packed.at[level, p], fibres.at[level, me], send_sems.at[sem], recv_sems.at[sem], {"gx": p})
            )
        fibres[level, me] = packed[level, me]
    for level in range(depth):
        for copy in copies[level * (n - 1) : (level + 1) * (n - 1)]:
            copy.wait()
        parts = parts_of(fibres[level].reshape(n * rows, width))
        for i, part in enumerate(parts):
            split[i, level] = part
        add_gram(gram, parts, level == 0)
    start_load.wait()


def second_exchange(n, cells, factor, split, rows_ref, gram, packed, land, send_sems, recv_sems):
    me = lax.axis_index("gy")
    depth, ranks, width = packed.shape[0], packed.shape[2], packed.shape[3]
    peers = partners(n, me)
    copies = []
    factor = parts_of(factor)
    for level in range(depth):
        field = [split[i, level] for i in range(len(factor))]
        packed[level] = dot_parts(factor, field, 1, 0).reshape(n, ranks, width)
        for turn, p in enumerate(peers):
            sem = level * (n - 1) + turn
            copies.append(
                send(packed.at[level, p], land.at[me, level], send_sems.at[sem], recv_sems.at[sem], {"gy": p})
            )
        land[me, level] = packed[level, me]
    lane_group = lax.shift_right_logical(
        lax.broadcasted_iota(jnp.int32, (ranks, LANES), 1), cells.bit_length() - 1
    )
    for level in range(depth):
        for copy in copies[level * (n - 1) : (level + 1) * (n - 1)]:
            copy.wait()
        chunks = width // LANES
        for tile in range(chunks):
            for s in range(n):
                merged = None
                for g in range(n):
                    t, chunk = divmod(n * tile + g, chunks)
                    turned = land[t, level, :, chunk * LANES : (chunk + 1) * LANES]
                    if g != s:
                        turned = pltpu.roll(turned, cells * ((g - s) % n), 1)
                    merged = turned if g == 0 else jnp.where(lane_group == g, turned, merged)
                rows_ref[s, level, :, tile * LANES : (tile + 1) * LANES] = merged
        if level % 2 or level == depth - 1:
            low = level - level % 2
            whole = rows_ref[:, low : level + 1].reshape(n * (level + 1 - low) * ranks, width)
            add_gram(gram, parts_of(whole.T), low == 0)


def flat_plan(rows, nx, ny, nz):
    piece = rows // (nx * ny * nz)
    count = nx * (nz - 1) + nx * ny - 1
    return (nz, nx, ny, piece, LANES), [
        pltpu.VMEM((nz - 1, nx, ny, piece, LANES), jnp.float32),
        pltpu.VMEM((nx, ny, piece, LANES), jnp.float32),
        pltpu.VMEM((nx, ny, piece, LANES), jnp.float32),
        pltpu.VMEM((nz, nx, ny, piece, LANES), jnp.float32),
        pltpu.SemaphoreType.DMA((2, count)),
        pltpu.SemaphoreType.DMA((2, count)),
    ]


def flat_reduce(nx, ny, nz, held, scratch):
    land_core, half, land, total, send_sems, recv_sems = scratch
    mx, my, mz = lax.axis_index("gx"), lax.axis_index("gy"), lax.axis_index("gz")
    cores, columns, planes = partners(nz, mz), partners(nx, mx), partners(ny, my)
    groups = columns + [mx]
    base = nx * (nz - 1)

    def turns(px):
        return [(px, py) for py in planes + ([] if px is mx else [my])]

    order = [(i, px, py) for i, (px, py) in enumerate(sum((turns(px) for px in groups), []))]

    across = []
    for i, px in enumerate(groups):
        across.append([
            send(held.at[p, px], land_core.at[d, px], send_sems.at[0, i * (nz - 1) + d],
                 recv_sems.at[0, i * (nz - 1) + d], {"gz": p})
            for d, p in enumerate(cores)
        ])
    copies = {}
    for i, px in enumerate(groups):
        for copy in across[i]:
            copy.wait()
        summed = held[mz, px]
        for d in range(nz - 1):
            summed = summed + land_core[d, px]
        half[px] = summed
        for slot, qx, qy in order:
            if qx is px:
                copies[slot] = send(half.at[qx, qy], land.at[mx, my], send_sems.at[0, base + slot],
                                    recv_sems.at[0, base + slot], {"gx": qx, "gy": qy})
    result = half[mx, my]
    for slot, qx, qy in reversed(order):
        copies[slot].wait()
        result = result + land[qx, qy]
    total[mz, mx, my] = result
    own = total.at[mz, mx, my]
    for slot, qx, qy in order:
        copies[slot] = send(own, own, send_sems.at[1, base + slot], recv_sems.at[1, base + slot], {"gx": qx, "gy": qy})
    across = []
    for i, px in reversed(list(enumerate(groups))):
        for slot, qx, qy in order:
            if qx is px:
                copies[slot].wait()
        block = total.at[mz, px]
        for d, p in enumerate(cores):
            across.append(send(block, block, send_sems.at[1, i * (nz - 1) + d], recv_sems.at[1, i * (nz - 1) + d], {"gz": p}))
    for copy in across:
        copy.wait()


def stages_kernel(axes, sizes, cells, x_ref, start_ref, factor_ref, rows_ref, gram_ref, *scratch):
    nz, ny, nx = sizes
    targets = axis_peers(axes, sizes)
    gram, field, fibres, packed, load_sems, send_first, recv_first = scratch[:7]
    packed_second, land, send_second, recv_second, start, start_sem, split = scratch[7:14]
    half = (len(scratch) - 14) // 2
    reduces = scratch[14 : 14 + half], scratch[14 + half :]
    start_load = pltpu.make_async_copy(start_ref, start, start_sem)

    def reduced(reduce_scratch, into):
        held, total = reduce_scratch[0], reduce_scratch[4]
        held[...] = gram[...].reshape(held.shape)
        flat_reduce(nx, ny, nz, held, reduce_scratch[1:])
        into[...] = total[...].reshape(into.shape)

    first_exchange(nx, targets, x_ref, start_load, field, fibres, split, gram, packed, load_sems, send_first, recv_first)
    reduced(reduces[0], gram)
    factor = power_steps(gram, start[...])
    factor_ref[...] = factor
    second_exchange(ny, cells, factor, split, rows_ref, gram, packed_second, land, send_second, recv_second)
    reduced(reduces[1], gram_ref)


def stages(field, start, axes, sizes, cells):
    nz, ny, nx = sizes
    depth, rows, columns = field.shape
    rank, extent = start.shape
    width = columns // nx
    ranks = rank // ny
    gram_shape = (len(upper_blocks(extent // LANES)) * LANES, LANES)
    blocked, reduce_scratch = flat_plan(gram_shape[0], nx, ny, nz)
    reduce_scratch = [pltpu.VMEM(blocked, jnp.float32)] + reduce_scratch
    first, second = depth * (nx - 1), depth * (ny - 1)
    return pl.pallas_call(
        functools.partial(stages_kernel, axes, sizes, cells),
        out_shape=(
            jax.ShapeDtypeStruct((rank, extent), jnp.float32),
            jax.ShapeDtypeStruct((ny, depth, ranks, width), jnp.float32),
            jax.ShapeDtypeStruct(gram_shape, jnp.float32),
        ),
        in_specs=[pl.BlockSpec(memory_space=pltpu.HBM)] * 2,
        out_specs=(VMEM, VMEM, VMEM),
        scratch_shapes=[
            pltpu.VMEM(gram_shape, jnp.float32),
            pltpu.VMEM((depth, rows, columns), jnp.float32),
            pltpu.VMEM((depth, nx, rows, width), jnp.float32),
            pltpu.VMEM((depth, nx, rows, width), jnp.float32),
            pltpu.SemaphoreType.DMA((depth,)),
            pltpu.SemaphoreType.DMA((first,)),
            pltpu.SemaphoreType.DMA((first,)),
            pltpu.VMEM((depth, ny, ranks, width), jnp.float32),
            pltpu.VMEM((ny, depth, ranks, width), jnp.float32),
            pltpu.SemaphoreType.DMA((second,)),
            pltpu.SemaphoreType.DMA((second,)),
            pltpu.VMEM((rank, extent), jnp.float32),
            pltpu.SemaphoreType.DMA,
            pltpu.VMEM((3, depth, extent, width), jnp.bfloat16),
            *reduce_scratch,
            *reduce_scratch,
        ],
        compiler_params=pltpu.CompilerParams(collective_id=0, has_side_effects=True, vmem_limit_bytes=GRANT),
    )(field, start)


def in_hbm(x):
    return pltpu.with_memory_space_constraint(x, pltpu.HBM)


def local(nx, ny, nz, species_field, start_first, start_second):
    depth, rows, columns = species_field.shape
    rank, extent = start_first.shape[1], start_second.shape[0]
    species, ranks = S // nx, rank // ny
    cells = LANES // species
    fits = (
        columns % (nx * LANES) == 0
        and columns // nx == extent
        and nx * rows == extent
        and species == ny
        and extent % LANES == 0
        and nx * rows % LANES == 0
        and ranks % 8 == 0
        and rank % 16 == 0
        and len(upper_blocks(extent // LANES)) * LANES % (8 * nx * ny * nz) == 0
    )
    if not fits:
        return local_general(nx, ny, nz, species_field, start_first, start_second)
    axes, sizes = ("gz", "gy", "gx"), (nz, ny, nx)
    factor_first, rows_second, gram_second = stages(in_hbm(species_field), in_hbm(start_first.T), axes, sizes, cells)
    rows_second = rows_second.reshape(species * depth * ranks, extent)
    factor_first, factor_second, core = pl.pallas_call(
        second_power_kernel,
        out_shape=(
            jax.ShapeDtypeStruct((rank, extent), jnp.float32),
            jax.ShapeDtypeStruct((rank, extent), jnp.float32),
            jax.ShapeDtypeStruct((rows_second.shape[0], rank), jnp.float32),
        ),
        in_specs=[VMEM, VMEM, VMEM, VMEM],
        out_specs=(VMEM, VMEM, VMEM),
        compiler_params=pltpu.CompilerParams(vmem_limit_bytes=GRANT),
    )(gram_second, start_second.T, rows_second, factor_first)
    return (factor_first.T, factor_second.T, core.reshape(species, depth, ranks, rank))


def solution(mesh):
    return jax.shard_map(
        functools.partial(local, mesh.shape["gx"], mesh.shape["gy"], mesh.shape["gz"]),
        mesh=mesh,
        in_specs=(P("gz", "gx", "gy"), P(), P()),
        out_specs=(P(), P(), P("gx", "gz", "gy", None)),
        check_vma=False,
    )
```

```python
import functools

import jax
import jax.numpy as jnp
from jax import lax
from jax.experimental import pallas as pl
from jax.experimental.pallas import tpu as pltpu
from jax.sharding import PartitionSpec as P

S = 16
ITERS = 2
LANES = 128
GRANT = 32 * 2**20
MESH = pl.DeviceIdType.MESH
VMEM = pl.BlockSpec(memory_space=pltpu.VMEM)

exact_precision = lax.Precision.HIGHEST


def dot_dims(a, b, contract_a, contract_b):
    return lax.dot_general(
        a, b, (((contract_a,), (contract_b,)), ((), ())),
        precision=exact_precision, preferred_element_type=jnp.float32,
    )


def partners(n, me):
    if n == 4:
        return [3 - me, lax.rem(me + 2, 4), me + 1 - 2 * lax.rem(me, 2)]
    return [lax.rem(me + d, n) for d in range(1, n)]


def far_partners(n, me):
    if n == 4:
        return [lax.rem(me + 2, 4), 3 - me, me + 1 - 2 * lax.rem(me, 2)]
    return partners(n, me)


def send(src, dst, send_sem, recv_sem, target):
    copy = pltpu.make_async_remote_copy(
        src_ref=src, dst_ref=dst, send_sem=send_sem, recv_sem=recv_sem,
        device_id=target, device_id_type=MESH,
    )
    copy.start()
    return copy


def say_hello(targets):
    barrier = pltpu.get_barrier_semaphore()
    for target in targets:
        pl.semaphore_signal(barrier, inc=1, device_id=target, device_id_type=MESH)


def hear_hello(targets):
    pl.semaphore_wait(pltpu.get_barrier_semaphore(), len(targets))


def greet(targets):
    say_hello(targets)
    hear_hello(targets)


def axis_peers(axes, sizes):
    return [{axis: p} for axis, n in zip(axes, sizes) for p in partners(n, lax.axis_index(axis))]


def reduce_blocks(axes, sizes, splits, x_ref, o_ref, scratch):
    levels = len(axes)
    landing, totals = scratch[:levels], scratch[levels : 2 * levels - 1]
    send_sems, recv_sems = scratch[2 * levels - 1 :]
    me = [lax.axis_index(axis) for axis in axes]
    peers = [partners(n, m) for n, m in zip(sizes, me)]
    spot = [m if split > 1 else 0 for m, split in zip(me, splits)]
    sem = 0
    held = x_ref
    for level in range(levels):
        axis, n, split = axes[level], sizes[level], splits[level]
        land = landing[level]
        copies = []
        for p in peers[level]:
            src = held.at[p] if split > 1 else held.at[0]
            copies.append(send(src, land.at[me[level]], send_sems.at[sem], recv_sems.at[sem], {axis: p}))
            sem += 1
        land[me[level]] = held[spot[level]]
        for copy in copies:
            copy.wait()
        total = land[0]
        for source in range(1, n):
            total = total + land[source]
        if level < levels - 1:
            totals[level][...] = total
            held = totals[level]
        else:
            o_ref[tuple(spot)] = total

    for level in reversed(range(levels)):
        if splits[level] == 1:
            continue
        block = o_ref.at[tuple(spot[: level + 1])]
        copies = []
        for p in peers[level]:
            copies.append(send(block, block, send_sems.at[sem], recv_sems.at[sem], {axes[level]: p}))
            sem += 1
        for copy in copies:
            copy.wait()


def all_reduce_kernel(axes, sizes, splits, x_ref, o_ref, *scratch):
    greet(axis_peers(axes, sizes))
    reduce_blocks(axes, sizes, splits, x_ref, o_ref, scratch)


def reduce_plan(rows, columns, sizes):
    splits = []
    for n in sizes:
        splits.append(n if rows % n == 0 else 1)
        rows //= splits[-1]
    scratch = [
        pltpu.VMEM((n, *splits[level + 1 :], rows, columns), jnp.float32)
        for level, n in enumerate(sizes)
    ]
    scratch += [pltpu.VMEM((*splits[level + 1 :], rows, columns), jnp.float32) for level in range(len(sizes) - 1)]
    count = sum(n - 1 for n in sizes) + sum(n - 1 for n, split in zip(sizes, splits) if split > 1)
    scratch += [pltpu.SemaphoreType.DMA((count,)), pltpu.SemaphoreType.DMA((count,))]
    return splits, (*splits, rows, columns), scratch


def all_reduce(x, axes, sizes, collective_id):
    splits, blocked, scratch = reduce_plan(*x.shape, sizes)
    out = pl.pallas_call(
        functools.partial(all_reduce_kernel, axes, sizes, splits),
        out_shape=jax.ShapeDtypeStruct(blocked, jnp.float32),
        in_specs=[VMEM],
        out_specs=VMEM,
        scratch_shapes=scratch,
        compiler_params=pltpu.CompilerParams(collective_id=collective_id, has_side_effects=True),
    )(x.reshape(blocked))
    return out.reshape(x.shape)


def fibres_kernel(n, x_ref, o_ref, send_sems, recv_sems):
    me = lax.axis_index("gx")
    depth, rows, width = x_ref.shape[0], x_ref.shape[1], o_ref.shape[-1]
    peers = partners(n, me)
    greet([{"gx": p} for p in peers])
    copies = []
    for turn, p in enumerate(peers):
        columns = pl.ds(pl.multiple_of(p * width, width), width)
        copies.append(
            send(x_ref.at[:, :, columns], o_ref.at[:, me], send_sems.at[turn], recv_sems.at[turn], {"gx": p})
        )
    own = pl.ds(pl.multiple_of(me * width, width), width)
    for level in range(depth):
        o_ref[level, me] = x_ref[level, :, own]
    for copy in copies:
        copy.wait()


def gather_fibres(field, n):
    depth, rows, columns = field.shape
    width = columns // n
    if width % 128:
        return lax.all_to_all(field, "gx", split_axis=2, concat_axis=1, tiled=True)
    out = pl.pallas_call(
        functools.partial(fibres_kernel, n),
        out_shape=jax.ShapeDtypeStruct((depth, n, rows, width), jnp.float32),
        in_specs=[VMEM],
        out_specs=VMEM,
        scratch_shapes=[pltpu.SemaphoreType.DMA((n - 1,)), pltpu.SemaphoreType.DMA((n - 1,))],
        compiler_params=pltpu.CompilerParams(collective_id=0, has_side_effects=True),
    )(field)
    return out.reshape(depth, n * rows, width)


def exchange_kernel(nx, ny, x_ref, o_ref, send_sems, recv_sems):
    mx, my = lax.axis_index("gx"), lax.axis_index("gy")
    peers = [(px, my) for px in partners(nx, mx)]
    for py in partners(ny, my):
        peers += [(px, py) for px in partners(nx, mx) + [mx]]
    greet([{"gx": px, "gy": py} for px, py in peers])
    copies = []
    for turn, (px, py) in enumerate(peers):
        copies.append(
            send(x_ref.at[py, px], o_ref.at[my, mx], send_sems.at[turn], recv_sems.at[turn], {"gx": px, "gy": py})
        )
    o_ref[my, mx] = x_ref[my, mx]
    for copy in copies:
        copy.wait()


def exchange(blocks):
    ny, nx = blocks.shape[:2]
    count = nx * ny - 1
    return pl.pallas_call(
        functools.partial(exchange_kernel, nx, ny),
        out_shape=jax.ShapeDtypeStruct(blocks.shape, jnp.float32),
        in_specs=[VMEM],
        out_specs=VMEM,
        scratch_shapes=[pltpu.SemaphoreType.DMA((count,)), pltpu.SemaphoreType.DMA((count,))],
        compiler_params=pltpu.CompilerParams(collective_id=1, has_side_effects=True),
    )(blocks)


def inverse_lower(cross):
    rank = cross.shape[0]
    groups = rank // 8
    local_row = lax.broadcasted_iota(jnp.int32, (8, rank), 0)
    lane = lax.broadcasted_iota(jnp.int32, (8, rank), 1)

    def row_of(block, r):
        return jnp.broadcast_to(block[r : r + 1], (8, rank))

    def column_of(block, c):
        return jnp.broadcast_to(block[:, c : c + 1], (8, rank))

    rest = [cross[8 * g : 8 * g + 8] for g in range(groups)]
    pivots = [column_of(rest[0], j) for j in range(8)]
    near = [column_of(rest[1], j) for j in range(8)] if groups > 1 else None
    done = []
    for k in range(groups):
        low = 8 * k
        next_pivots = [column_of(rest[k + 1], low + 8 + j) for j in range(8)] if k + 1 < groups else None
        next_near = [column_of(rest[k + 2], low + 8 + j) for j in range(8)] if k + 2 < groups else None
        columns = {(j, k + 1): near[j] for j in range(8)} if k + 1 < groups else {}
        for g in range(k + 2, groups):
            for j in range(8):
                columns[j, g] = column_of(rest[g], low + j)
        own_lanes = (lane >= low) & (lane < low + 8)
        rest[k] = jnp.where(own_lanes, jnp.where(lane == local_row + low, 1.0, 0.0), rest[k])
        for g in range(k + 1, groups):
            rest[g] = jnp.where(own_lanes, 0.0, rest[g])
        diagonal = jnp.ones((8, rank), jnp.float32)
        factors = []
        for j in range(8):
            pivot = row_of(pivots[j], j)
            diagonal = jnp.where(local_row == j, pivot, diagonal)
            reciprocal = 1.0 / pivot
            factor = pivots[j] * reciprocal
            factors.append(factor)
            values = {other: row_of(pivots[j], other) for other in range(j + 1, 8)}
            for other in range(j + 1, 8):
                if other == j + 1:
                    change = (pivots[j] * values[other]) * reciprocal
                else:
                    change = factor * values[other]
                pivots[other] = pivots[other] - change
            own_row = row_of(rest[k], j)
            rest[k] = rest[k] - jnp.where(local_row > j, factor, 0.0) * own_row
            if k + 1 < groups:
                ahead = [row_of(columns[j, k + 1], other) for other in range(8)]
            for g in range(k + 1, min(k + 3, groups)):
                factor = columns[j, g] * reciprocal
                for other in range(j + 1, 8):
                    columns[other, g] = columns[other, g] - factor * values[other]
                following = next_pivots if g == k + 1 else next_near
                for other in range(8):
                    following[other] = following[other] - factor * ahead[other]
                rest[g] = rest[g] - factor * own_row
        done.append(jnp.where(lane < low + 8, rest[k] * (1.0 / jnp.sqrt(diagonal)), 0.0))
        if k + 3 < groups:
            solved = rest[k] * (1.0 / diagonal)
            for j in range(7, 0, -1):
                above = jnp.zeros((8, rank), jnp.float32)
                for i in range(j):
                    above = jnp.where(local_row == i, row_of(factors[i], j), above)
                solved = solved - above * row_of(solved, j)
            for j in range(8):
                own_row = row_of(solved, j)
                for g in range(k + 3, groups):
                    rest[g] = rest[g] - columns[j, g] * own_row
        pivots, near = next_pivots, next_near
    return jnp.concatenate(done, axis=0)


def power_general_kernel(gram_ref, start_ref, out_ref):
    current = start_ref[...]
    for turn in range(ITERS):
        images = dot_dims(gram_ref[...], current, 1, 0)
        cross = dot_dims(images, images, 0, 0)
        current = dot_dims(images, inverse_lower(cross), 1, 1)
    out_ref[...] = current


def leading(gram, start):
    return pl.pallas_call(
        power_general_kernel,
        out_shape=jax.ShapeDtypeStruct(start.shape, jnp.float32),
        in_specs=[VMEM, VMEM],
        out_specs=VMEM,
    )(gram, start)


def local_general(nx, ny, nz, species_field, start_first, start_second):
    axes, sizes = ("gz", "gy", "gx"), (nz, ny, nx)
    fibres = gather_fibres(species_field, nx)
    partial_gram = jnp.einsum("zic,zjc->ij", fibres, fibres, precision=exact_precision)
    gram_first = all_reduce(partial_gram, axes, sizes, 2)
    factor_first = leading(gram_first, start_first)

    depth = fibres.shape[0]
    cells = fibres.shape[2] // S
    rank = start_first.shape[1]
    species, ranks = S // nx, rank // ny
    projected = jnp.einsum("zim,ir->zmr", fibres, factor_first, precision=exact_precision)
    blocks = projected.reshape(depth, cells, nx, species, ny, ranks)
    blocks = blocks.transpose(4, 2, 1, 3, 0, 5).reshape(ny, nx, cells, species * depth * ranks)
    columns = exchange(blocks)
    columns = columns.reshape(ny * nx * cells, species * depth * ranks)
    partial_second = dot_dims(columns, columns, 1, 1)
    gram_second = all_reduce(partial_second, axes, sizes, 3)
    factor_second = leading(gram_second, start_second)
    core = dot_dims(columns, factor_second, 0, 0)
    core = core.reshape(species, depth, ranks, factor_second.shape[1])
    return (factor_first, factor_second, core)


def upper_blocks(count):
    return [(a, b) for a in range(count) for b in range(a, count)]


def parts_of(x):
    high = x.astype(jnp.bfloat16)
    left = x - high.astype(jnp.float32)
    middle = left.astype(jnp.bfloat16)
    return high, middle, (left - middle.astype(jnp.float32)).astype(jnp.bfloat16)


def dot_parts(a, b, contract_a, contract_b):
    a, b = tuple(a), tuple(b)
    rows = a[0].shape[0]

    def dot(x, y):
        return lax.dot_general(
            x, y, (((contract_a,), (contract_b,)), ((), ())), preferred_element_type=jnp.float32
        )

    by_high = dot(jnp.concatenate(a, axis=0), b[0])
    by_middle = dot(jnp.concatenate(a[:2], axis=0), b[1])
    small = by_high[2 * rows :] + by_middle[rows:] + dot(a[0], b[2])
    return (small + (by_high[rows : 2 * rows] + by_middle[:rows])) + by_high[:rows]


def add_gram(gram_ref, parts, first, slots=None):
    blocks = upper_blocks(parts[0].shape[0] // LANES)
    slots = range(len(blocks)) if slots is None else slots
    for a in sorted({blocks[slot][0] for slot in slots}):
        row = [slot for slot in slots if blocks[slot][0] == a]
        low, high = blocks[row[0]][1] * LANES, (blocks[row[-1]][1] + 1) * LANES
        terms = dot_parts([x[a * LANES : (a + 1) * LANES] for x in parts], [x[low:high] for x in parts], 1, 1)
        for place, slot in enumerate(row):
            block = pl.ds(slot * LANES, LANES)
            term = terms[:, place * LANES : (place + 1) * LANES]
            gram_ref[block, :] = term if first else gram_ref[block, :] + term


def finish_gram(held, across, gram_ref, load_parts, first):
    nz = held.shape[0]
    count = gram_ref.shape[0] // LANES

    def start():
        for copies in across:
            for copy in copies:
                copy.start()

    if nz != 2 or count % 2:
        add_gram(gram_ref, load_parts(), first)
        held[...] = gram_ref[...].reshape(held.shape)
        start()
        return

    def half(side):
        slots = range(side * count // 2, (side + 1) * count // 2)
        add_gram(gram_ref, load_parts(), first, slots)
        rows = gram_ref[slots[0] * LANES : (slots[-1] + 1) * LANES, :]
        held[side] = rows.reshape(held.shape[1:])

    def mine_last(side):
        def body():
            half(1 - side)
            start()
            half(side)

        return body

    mz = lax.axis_index("gz")
    for side in range(2):
        pl.when(mz == side)(mine_last(side))


def whole_gram(gram):
    count = 1
    while count * (count + 1) // 2 * LANES < gram.shape[0]:
        count += 1
    block = {}
    for slot, (a, b) in enumerate(upper_blocks(count)):
        block[a, b] = gram[slot * LANES : (slot + 1) * LANES, :]
        if a != b:
            block[b, a] = block[a, b].T
    return jnp.concatenate(
        [jnp.concatenate([block[a, b] for b in range(count)], axis=1) for a in range(count)], axis=0
    )


def last_images(gram_ref, current):
    gram = parts_of(whole_gram(gram_ref[...]))
    for turn in range(ITERS):
        images = parts_of(dot_parts(parts_of(current), gram, 1, 0))
        inverse = parts_of(inverse_lower(dot_parts(images, images, 1, 1)))
        if turn < ITERS - 1:
            current = dot_parts(inverse, images, 1, 0)
    return images, inverse


def power_steps(gram_ref, current):
    images, inverse = last_images(gram_ref, current)
    return dot_parts(inverse, images, 1, 0)


def second_power_kernel(gram_ref, start_ref, rows_ref, first_ref, first_out_ref, out_ref, core_ref):
    first_out_ref[...] = first_ref[...]
    images, inverse = last_images(gram_ref, start_ref[...])
    on_images = parts_of(dot_parts(parts_of(rows_ref[...]), images, 1, 1))
    out_ref[...] = dot_parts(inverse, images, 1, 0)
    core_ref[...] = dot_parts(on_images, inverse, 1, 1)


def species_major(block, order):
    high = block.astype(jnp.bfloat16)
    left = block - high.astype(jnp.float32)
    middle = left.astype(jnp.bfloat16)
    low = (left - middle.astype(jnp.float32)).astype(jnp.bfloat16)
    moved = [
        lax.dot_general(part, order, (((1,), (0,)), ((), ())), preferred_element_type=jnp.float32)
        for part in (high, middle, low)
    ]
    return (moved[0] + moved[1]) + moved[2]


def first_exchange(n, targets, finish, x_ref, start_load, field, fibres, split, gram, packed, load_sems, send_sems, recv_sems):
    me = lax.axis_index("gx")
    depth, rows, columns = field.shape
    span = n * LANES
    cells = span // S
    width = columns // n
    loads = [pltpu.make_async_copy(x_ref.at[z], field.at[z], load_sems.at[z]) for z in range(depth)]
    for load in loads + [start_load]:
        load.start()
    say_hello(targets)
    peers = far_partners(n, me)
    source = lax.broadcasted_iota(jnp.int32, (span, span), 0)
    target = lax.broadcasted_iota(jnp.int32, (span, span), 1)
    species = lax.shift_right_logical(target, cells.bit_length() - 1)
    order = jnp.where(source == (target & (cells - 1)) * S + species, 1.0, 0.0).astype(jnp.bfloat16)
    copies = []
    for level in range(depth):
        loads[level].wait()
        for chunk in range(columns // span):
            moved = species_major(field[level, :, chunk * span : (chunk + 1) * span], order)
            lanes = pl.ds(chunk * LANES, LANES)
            for p in range(n):
                packed[level, p, :, lanes] = moved[:, p * LANES : (p + 1) * LANES]
        if level == 0:
            hear_hello(targets)
        for turn, p in enumerate(peers):
            sem = level * (n - 1) + turn
            copies.append(
                send(packed.at[level, p], fibres.at[level, me], send_sems.at[sem], recv_sems.at[sem], {"gx": p})
            )
        fibres[level, me] = packed[level, me]
    for level in range(depth):
        for copy in copies[level * (n - 1) : (level + 1) * (n - 1)]:
            copy.wait()
        parts = parts_of(fibres[level].reshape(n * rows, width))
        for i, part in enumerate(parts):
            split[i, level] = part
        if level < depth - 1:
            add_gram(gram, parts, level == 0)
    finish(gram, lambda: [split[i, depth - 1] for i in range(3)], depth == 1)
    start_load.wait()


def second_exchange(n, cells, finish, factor, split, last, rows_ref, gram, packed, land, send_sems, recv_sems):
    me = lax.axis_index("gy")
    depth, ranks, width = packed.shape[0], packed.shape[2], packed.shape[3]
    peers = partners(n, me)
    copies = []
    factor = parts_of(factor)
    for level in range(depth):
        field = [split[i, level] for i in range(len(factor))]
        packed[level] = dot_parts(factor, field, 1, 0).reshape(n, ranks, width)
        for turn, p in enumerate(peers):
            sem = level * (n - 1) + turn
            copies.append(
                send(packed.at[level, p], land.at[me, level], send_sems.at[sem], recv_sems.at[sem], {"gy": p})
            )
        land[me, level] = packed[level, me]
    lane_group = lax.shift_right_logical(
        lax.broadcasted_iota(jnp.int32, (ranks, LANES), 1), cells.bit_length() - 1
    )
    for level in range(depth):
        for copy in copies[level * (n - 1) : (level + 1) * (n - 1)]:
            copy.wait()
        chunks = width // LANES
        for tile in range(chunks):
            for s in range(n):
                merged = None
                for g in range(n):
                    t, chunk = divmod(n * tile + g, chunks)
                    turned = land[t, level, :, chunk * LANES : (chunk + 1) * LANES]
                    if g != s:
                        turned = pltpu.roll(turned, cells * ((g - s) % n), 1)
                    merged = turned if g == 0 else jnp.where(lane_group == g, turned, merged)
                rows_ref[s, level, :, tile * LANES : (tile + 1) * LANES] = merged
        if level % 2 or level == depth - 1:
            low = level - level % 2
            whole = rows_ref[:, low : level + 1].reshape(n * (level + 1 - low) * ranks, width)
            parts = parts_of(whole.T)
            if level < depth - 1:
                add_gram(gram, parts, low == 0)
            else:
                for i, part in enumerate(parts):
                    last[i] = part
                finish(gram, lambda: [last[i] for i in range(3)], low == 0)


def flat_plan(rows, nx, ny, nz):
    piece = rows // (nx * ny * nz)
    count = nx * (nz - 1) + nx * ny - 1
    return (nz, nx, ny, piece, LANES), [
        pltpu.VMEM((nz - 1, nx, ny, piece, LANES), jnp.float32),
        pltpu.VMEM((nx, ny, piece, LANES), jnp.float32),
        pltpu.VMEM((nx, ny, piece, LANES), jnp.float32),
        pltpu.VMEM((nz, nx, ny, piece, LANES), jnp.float32),
        pltpu.SemaphoreType.DMA((2, count)),
        pltpu.SemaphoreType.DMA((2, count)),
    ]


def across_copies(nx, nz, held, scratch):
    land_core, send_sems, recv_sems = scratch[0], scratch[4], scratch[5]
    mx, mz = lax.axis_index("gx"), lax.axis_index("gz")
    copies = []
    for i, px in enumerate(partners(nx, mx) + [mx]):
        copies.append([])
        for d, p in enumerate(partners(nz, mz)):
            sem = i * (nz - 1) + d
            copies[-1].append(pltpu.make_async_remote_copy(
                src_ref=held.at[p, px], dst_ref=land_core.at[d, px], send_sem=send_sems.at[0, sem],
                recv_sem=recv_sems.at[0, sem], device_id={"gz": p}, device_id_type=MESH,
            ))
    return copies


def flat_reduce(nx, ny, nz, held, across, scratch):
    land_core, half, land, total, send_sems, recv_sems = scratch
    mx, my, mz = lax.axis_index("gx"), lax.axis_index("gy"), lax.axis_index("gz")
    cores, columns, planes = partners(nz, mz), partners(nx, mx), partners(ny, my)
    groups = columns + [mx]
    base = nx * (nz - 1)

    def turns(px):
        return [(px, py) for py in planes + ([] if px is mx else [my])]

    order = [(i, px, py) for i, (px, py) in enumerate(sum((turns(px) for px in groups), []))]

    copies = {}
    for i, px in enumerate(groups):
        for copy in across[i]:
            copy.wait()
        summed = held[mz, px]
        for d in range(nz - 1):
            summed = summed + land_core[d, px]
        half[px] = summed
        for slot, qx, qy in order:
            if qx is px:
                copies[slot] = send(half.at[qx, qy], land.at[mx, my], send_sems.at[0, base + slot],
                                    recv_sems.at[0, base + slot], {"gx": qx, "gy": qy})
    result = half[mx, my]
    for slot, qx, qy in reversed(order):
        copies[slot].wait()
        result = result + land[qx, qy]
    total[mz, mx, my] = result
    own = total.at[mz, mx, my]
    for slot, qx, qy in order:
        copies[slot] = send(own, own, send_sems.at[1, base + slot], recv_sems.at[1, base + slot], {"gx": qx, "gy": qy})
    across = []
    for i, px in reversed(list(enumerate(groups))):
        for slot, qx, qy in order:
            if qx is px:
                copies[slot].wait()
        block = total.at[mz, px]
        for d, p in enumerate(cores):
            across.append(send(block, block, send_sems.at[1, i * (nz - 1) + d], recv_sems.at[1, i * (nz - 1) + d], {"gz": p}))
    for copy in across:
        copy.wait()


def stages_kernel(axes, sizes, cells, x_ref, start_ref, factor_ref, rows_ref, gram_ref, *scratch):
    nz, ny, nx = sizes
    targets = axis_peers(axes, sizes)
    gram, field, fibres, packed, load_sems, send_first, recv_first = scratch[:7]
    packed_second, land, send_second, recv_second, start, start_sem, split, last = scratch[7:15]
    half = (len(scratch) - 15) // 2
    reduces = scratch[15 : 15 + half], scratch[15 + half :]
    start_load = pltpu.make_async_copy(start_ref, start, start_sem)

    across = [across_copies(nx, nz, reduce[0], reduce[1:]) for reduce in reduces]
    finish = [functools.partial(finish_gram, reduce[0], copies) for reduce, copies in zip(reduces, across)]

    def reduced(turn, into):
        held, total = reduces[turn][0], reduces[turn][4]
        flat_reduce(nx, ny, nz, held, across[turn], reduces[turn][1:])
        into[...] = total[...].reshape(into.shape)

    first_exchange(nx, targets, finish[0], x_ref, start_load, field, fibres, split, gram, packed, load_sems, send_first, recv_first)
    reduced(0, gram)
    factor = power_steps(gram, start[...])
    factor_ref[...] = factor
    second_exchange(ny, cells, finish[1], factor, split, last, rows_ref, gram, packed_second, land, send_second, recv_second)
    reduced(1, gram_ref)


def stages(field, start, axes, sizes, cells):
    nz, ny, nx = sizes
    depth, rows, columns = field.shape
    rank, extent = start.shape
    width = columns // nx
    ranks = rank // ny
    gram_shape = (len(upper_blocks(extent // LANES)) * LANES, LANES)
    blocked, reduce_scratch = flat_plan(gram_shape[0], nx, ny, nz)
    reduce_scratch = [pltpu.VMEM(blocked, jnp.float32)] + reduce_scratch
    first, second = depth * (nx - 1), depth * (ny - 1)
    return pl.pallas_call(
        functools.partial(stages_kernel, axes, sizes, cells),
        out_shape=(
            jax.ShapeDtypeStruct((rank, extent), jnp.float32),
            jax.ShapeDtypeStruct((ny, depth, ranks, width), jnp.float32),
            jax.ShapeDtypeStruct(gram_shape, jnp.float32),
        ),
        in_specs=[pl.BlockSpec(memory_space=pltpu.HBM)] * 2,
        out_specs=(VMEM, VMEM, VMEM),
        scratch_shapes=[
            pltpu.VMEM(gram_shape, jnp.float32),
            pltpu.VMEM((depth, rows, columns), jnp.float32),
            pltpu.VMEM((depth, nx, rows, width), jnp.float32),
            pltpu.VMEM((depth, nx, rows, width), jnp.float32),
            pltpu.SemaphoreType.DMA((depth,)),
            pltpu.SemaphoreType.DMA((first,)),
            pltpu.SemaphoreType.DMA((first,)),
            pltpu.VMEM((depth, ny, ranks, width), jnp.float32),
            pltpu.VMEM((ny, depth, ranks, width), jnp.float32),
            pltpu.SemaphoreType.DMA((second,)),
            pltpu.SemaphoreType.DMA((second,)),
            pltpu.VMEM((rank, extent), jnp.float32),
            pltpu.SemaphoreType.DMA,
            pltpu.VMEM((3, depth, extent, width), jnp.bfloat16),
            pltpu.VMEM((3, width, (2 - depth % 2) * rank), jnp.bfloat16),
            *reduce_scratch,
            *reduce_scratch,
        ],
        compiler_params=pltpu.CompilerParams(collective_id=0, has_side_effects=True, vmem_limit_bytes=GRANT),
    )(field, start)


def in_hbm(x):
    return pltpu.with_memory_space_constraint(x, pltpu.HBM)


def local(nx, ny, nz, species_field, start_first, start_second):
    depth, rows, columns = species_field.shape
    rank, extent = start_first.shape[1], start_second.shape[0]
    species, ranks = S // nx, rank // ny
    cells = LANES // species
    fits = (
        columns % (nx * LANES) == 0
        and columns // nx == extent
        and nx * rows == extent
        and species == ny
        and extent % LANES == 0
        and nx * rows % LANES == 0
        and ranks % 8 == 0
        and rank % 16 == 0
        and len(upper_blocks(extent // LANES)) * LANES % (8 * nx * ny * nz) == 0
    )
    if not fits:
        return local_general(nx, ny, nz, species_field, start_first, start_second)
    axes, sizes = ("gz", "gy", "gx"), (nz, ny, nx)
    factor_first, rows_second, gram_second = stages(in_hbm(species_field), in_hbm(start_first.T), axes, sizes, cells)
    rows_second = rows_second.reshape(species * depth * ranks, extent)
    factor_first, factor_second, core = pl.pallas_call(
        second_power_kernel,
        out_shape=(
            jax.ShapeDtypeStruct((rank, extent), jnp.float32),
            jax.ShapeDtypeStruct((rank, extent), jnp.float32),
            jax.ShapeDtypeStruct((rows_second.shape[0], rank), jnp.float32),
        ),
        in_specs=[VMEM, VMEM, VMEM, VMEM],
        out_specs=(VMEM, VMEM, VMEM),
        compiler_params=pltpu.CompilerParams(vmem_limit_bytes=GRANT),
    )(gram_second, start_second.T, rows_second, factor_first)
    return (factor_first.T, factor_second.T, core.reshape(species, depth, ranks, rank))


def solution(mesh):
    return jax.shard_map(
        functools.partial(local, mesh.shape["gx"], mesh.shape["gy"], mesh.shape["gz"]),
        mesh=mesh,
        in_specs=(P("gz", "gx", "gy"), P(), P()),
        out_specs=(P(), P(), P("gx", "gz", "gy", None)),
        check_vma=False,
    )
```

```python
import functools

import jax
import jax.numpy as jnp
from jax import lax
from jax.experimental import pallas as pl
from jax.experimental.pallas import tpu as pltpu
from jax.sharding import PartitionSpec as P

S = 16
ITERS = 2
LANES = 128
GRANT = 32 * 2**20
MESH = pl.DeviceIdType.MESH
VMEM = pl.BlockSpec(memory_space=pltpu.VMEM)

exact_precision = lax.Precision.HIGHEST


def dot_dims(a, b, contract_a, contract_b):
    return lax.dot_general(
        a, b, (((contract_a,), (contract_b,)), ((), ())),
        precision=exact_precision, preferred_element_type=jnp.float32,
    )


def partners(n, me):
    if n == 4:
        return [3 - me, lax.rem(me + 2, 4), me + 1 - 2 * lax.rem(me, 2)]
    return [lax.rem(me + d, n) for d in range(1, n)]


def far_partners(n, me):
    if n == 4:
        return [lax.rem(me + 2, 4), 3 - me, me + 1 - 2 * lax.rem(me, 2)]
    return partners(n, me)


def send(src, dst, send_sem, recv_sem, target):
    copy = pltpu.make_async_remote_copy(
        src_ref=src, dst_ref=dst, send_sem=send_sem, recv_sem=recv_sem,
        device_id=target, device_id_type=MESH,
    )
    copy.start()
    return copy


def say_hello(targets):
    barrier = pltpu.get_barrier_semaphore()
    for target in targets:
        pl.semaphore_signal(barrier, inc=1, device_id=target, device_id_type=MESH)


def hear_hello(targets):
    pl.semaphore_wait(pltpu.get_barrier_semaphore(), len(targets))


def greet(targets):
    say_hello(targets)
    hear_hello(targets)


def axis_peers(axes, sizes):
    return [{axis: p} for axis, n in zip(axes, sizes) for p in partners(n, lax.axis_index(axis))]


def reduce_blocks(axes, sizes, splits, x_ref, o_ref, scratch):
    levels = len(axes)
    landing, totals = scratch[:levels], scratch[levels : 2 * levels - 1]
    send_sems, recv_sems = scratch[2 * levels - 1 :]
    me = [lax.axis_index(axis) for axis in axes]
    peers = [partners(n, m) for n, m in zip(sizes, me)]
    spot = [m if split > 1 else 0 for m, split in zip(me, splits)]
    sem = 0
    held = x_ref
    for level in range(levels):
        axis, n, split = axes[level], sizes[level], splits[level]
        land = landing[level]
        copies = []
        for p in peers[level]:
            src = held.at[p] if split > 1 else held.at[0]
            copies.append(send(src, land.at[me[level]], send_sems.at[sem], recv_sems.at[sem], {axis: p}))
            sem += 1
        land[me[level]] = held[spot[level]]
        for copy in copies:
            copy.wait()
        total = land[0]
        for source in range(1, n):
            total = total + land[source]
        if level < levels - 1:
            totals[level][...] = total
            held = totals[level]
        else:
            o_ref[tuple(spot)] = total

    for level in reversed(range(levels)):
        if splits[level] == 1:
            continue
        block = o_ref.at[tuple(spot[: level + 1])]
        copies = []
        for p in peers[level]:
            copies.append(send(block, block, send_sems.at[sem], recv_sems.at[sem], {axes[level]: p}))
            sem += 1
        for copy in copies:
            copy.wait()


def all_reduce_kernel(axes, sizes, splits, x_ref, o_ref, *scratch):
    greet(axis_peers(axes, sizes))
    reduce_blocks(axes, sizes, splits, x_ref, o_ref, scratch)


def reduce_plan(rows, columns, sizes):
    splits = []
    for n in sizes:
        splits.append(n if rows % n == 0 else 1)
        rows //= splits[-1]
    scratch = [
        pltpu.VMEM((n, *splits[level + 1 :], rows, columns), jnp.float32)
        for level, n in enumerate(sizes)
    ]
    scratch += [pltpu.VMEM((*splits[level + 1 :], rows, columns), jnp.float32) for level in range(len(sizes) - 1)]
    count = sum(n - 1 for n in sizes) + sum(n - 1 for n, split in zip(sizes, splits) if split > 1)
    scratch += [pltpu.SemaphoreType.DMA((count,)), pltpu.SemaphoreType.DMA((count,))]
    return splits, (*splits, rows, columns), scratch


def all_reduce(x, axes, sizes, collective_id):
    splits, blocked, scratch = reduce_plan(*x.shape, sizes)
    out = pl.pallas_call(
        functools.partial(all_reduce_kernel, axes, sizes, splits),
        out_shape=jax.ShapeDtypeStruct(blocked, jnp.float32),
        in_specs=[VMEM],
        out_specs=VMEM,
        scratch_shapes=scratch,
        compiler_params=pltpu.CompilerParams(collective_id=collective_id, has_side_effects=True),
    )(x.reshape(blocked))
    return out.reshape(x.shape)


def fibres_kernel(n, x_ref, o_ref, send_sems, recv_sems):
    me = lax.axis_index("gx")
    depth, rows, width = x_ref.shape[0], x_ref.shape[1], o_ref.shape[-1]
    peers = partners(n, me)
    greet([{"gx": p} for p in peers])
    copies = []
    for turn, p in enumerate(peers):
        columns = pl.ds(pl.multiple_of(p * width, width), width)
        copies.append(
            send(x_ref.at[:, :, columns], o_ref.at[:, me], send_sems.at[turn], recv_sems.at[turn], {"gx": p})
        )
    own = pl.ds(pl.multiple_of(me * width, width), width)
    for level in range(depth):
        o_ref[level, me] = x_ref[level, :, own]
    for copy in copies:
        copy.wait()


def gather_fibres(field, n):
    depth, rows, columns = field.shape
    width = columns // n
    if width % 128:
        return lax.all_to_all(field, "gx", split_axis=2, concat_axis=1, tiled=True)
    out = pl.pallas_call(
        functools.partial(fibres_kernel, n),
        out_shape=jax.ShapeDtypeStruct((depth, n, rows, width), jnp.float32),
        in_specs=[VMEM],
        out_specs=VMEM,
        scratch_shapes=[pltpu.SemaphoreType.DMA((n - 1,)), pltpu.SemaphoreType.DMA((n - 1,))],
        compiler_params=pltpu.CompilerParams(collective_id=0, has_side_effects=True),
    )(field)
    return out.reshape(depth, n * rows, width)


def exchange_kernel(nx, ny, x_ref, o_ref, send_sems, recv_sems):
    mx, my = lax.axis_index("gx"), lax.axis_index("gy")
    peers = [(px, my) for px in partners(nx, mx)]
    for py in partners(ny, my):
        peers += [(px, py) for px in partners(nx, mx) + [mx]]
    greet([{"gx": px, "gy": py} for px, py in peers])
    copies = []
    for turn, (px, py) in enumerate(peers):
        copies.append(
            send(x_ref.at[py, px], o_ref.at[my, mx], send_sems.at[turn], recv_sems.at[turn], {"gx": px, "gy": py})
        )
    o_ref[my, mx] = x_ref[my, mx]
    for copy in copies:
        copy.wait()


def exchange(blocks):
    ny, nx = blocks.shape[:2]
    count = nx * ny - 1
    return pl.pallas_call(
        functools.partial(exchange_kernel, nx, ny),
        out_shape=jax.ShapeDtypeStruct(blocks.shape, jnp.float32),
        in_specs=[VMEM],
        out_specs=VMEM,
        scratch_shapes=[pltpu.SemaphoreType.DMA((count,)), pltpu.SemaphoreType.DMA((count,))],
        compiler_params=pltpu.CompilerParams(collective_id=1, has_side_effects=True),
    )(blocks)


def inverse_lower(cross):
    rank = cross.shape[0]
    groups = rank // 8
    local_row = lax.broadcasted_iota(jnp.int32, (8, rank), 0)
    lane = lax.broadcasted_iota(jnp.int32, (8, rank), 1)

    def row_of(block, r):
        return jnp.broadcast_to(block[r : r + 1], (8, rank))

    def column_of(block, c):
        return jnp.broadcast_to(block[:, c : c + 1], (8, rank))

    rest = [cross[8 * g : 8 * g + 8] for g in range(groups)]
    pivots = [column_of(rest[0], j) for j in range(8)]
    near = [column_of(rest[1], j) for j in range(8)] if groups > 1 else None
    done = []
    for k in range(groups):
        low = 8 * k
        next_pivots = [column_of(rest[k + 1], low + 8 + j) for j in range(8)] if k + 1 < groups else None
        next_near = [column_of(rest[k + 2], low + 8 + j) for j in range(8)] if k + 2 < groups else None
        columns = {(j, k + 1): near[j] for j in range(8)} if k + 1 < groups else {}
        for g in range(k + 2, groups):
            for j in range(8):
                columns[j, g] = column_of(rest[g], low + j)
        own_lanes = (lane >= low) & (lane < low + 8)
        rest[k] = jnp.where(own_lanes, jnp.where(lane == local_row + low, 1.0, 0.0), rest[k])
        for g in range(k + 1, groups):
            rest[g] = jnp.where(own_lanes, 0.0, rest[g])
        diagonal = jnp.ones((8, rank), jnp.float32)
        factors = []
        for j in range(8):
            pivot = row_of(pivots[j], j)
            diagonal = jnp.where(local_row == j, pivot, diagonal)
            reciprocal = 1.0 / pivot
            factor = pivots[j] * reciprocal
            factors.append(factor)
            values = {other: row_of(pivots[j], other) for other in range(j + 1, 8)}
            for other in range(j + 1, 8):
                if other == j + 1:
                    change = (pivots[j] * values[other]) * reciprocal
                else:
                    change = factor * values[other]
                pivots[other] = pivots[other] - change
            own_row = row_of(rest[k], j)
            rest[k] = rest[k] - jnp.where(local_row > j, factor, 0.0) * own_row
            if k + 1 < groups:
                ahead = [row_of(columns[j, k + 1], other) for other in range(8)]
            for g in range(k + 1, min(k + 3, groups)):
                factor = columns[j, g] * reciprocal
                for other in range(j + 1, 8):
                    columns[other, g] = columns[other, g] - factor * values[other]
                following = next_pivots if g == k + 1 else next_near
                for other in range(8):
                    following[other] = following[other] - factor * ahead[other]
                rest[g] = rest[g] - factor * own_row
        done.append(jnp.where(lane < low + 8, rest[k] * (1.0 / jnp.sqrt(diagonal)), 0.0))
        if k + 3 < groups:
            solved = rest[k] * (1.0 / diagonal)
            for j in range(7, 0, -1):
                above = jnp.zeros((8, rank), jnp.float32)
                for i in range(j):
                    above = jnp.where(local_row == i, row_of(factors[i], j), above)
                solved = solved - above * row_of(solved, j)
            for j in range(8):
                own_row = row_of(solved, j)
                for g in range(k + 3, groups):
                    rest[g] = rest[g] - columns[j, g] * own_row
        pivots, near = next_pivots, next_near
    return jnp.concatenate(done, axis=0)


def power_general_kernel(gram_ref, start_ref, out_ref):
    current = start_ref[...]
    for turn in range(ITERS):
        images = dot_dims(gram_ref[...], current, 1, 0)
        cross = dot_dims(images, images, 0, 0)
        current = dot_dims(images, inverse_lower(cross), 1, 1)
    out_ref[...] = current


def leading(gram, start):
    return pl.pallas_call(
        power_general_kernel,
        out_shape=jax.ShapeDtypeStruct(start.shape, jnp.float32),
        in_specs=[VMEM, VMEM],
        out_specs=VMEM,
    )(gram, start)


def local_general(nx, ny, nz, species_field, start_first, start_second):
    axes, sizes = ("gz", "gy", "gx"), (nz, ny, nx)
    fibres = gather_fibres(species_field, nx)
    partial_gram = jnp.einsum("zic,zjc->ij", fibres, fibres, precision=exact_precision)
    gram_first = all_reduce(partial_gram, axes, sizes, 2)
    factor_first = leading(gram_first, start_first)

    depth = fibres.shape[0]
    cells = fibres.shape[2] // S
    rank = start_first.shape[1]
    species, ranks = S // nx, rank // ny
    projected = jnp.einsum("zim,ir->zmr", fibres, factor_first, precision=exact_precision)
    blocks = projected.reshape(depth, cells, nx, species, ny, ranks)
    blocks = blocks.transpose(4, 2, 1, 3, 0, 5).reshape(ny, nx, cells, species * depth * ranks)
    columns = exchange(blocks)
    columns = columns.reshape(ny * nx * cells, species * depth * ranks)
    partial_second = dot_dims(columns, columns, 1, 1)
    gram_second = all_reduce(partial_second, axes, sizes, 3)
    factor_second = leading(gram_second, start_second)
    core = dot_dims(columns, factor_second, 0, 0)
    core = core.reshape(species, depth, ranks, factor_second.shape[1])
    return (factor_first, factor_second, core)


def upper_blocks(count):
    return [(a, b) for a in range(count) for b in range(a, count)]


def parts_of(x):
    high = x.astype(jnp.bfloat16)
    left = x - high.astype(jnp.float32)
    middle = left.astype(jnp.bfloat16)
    return high, middle, (left - middle.astype(jnp.float32)).astype(jnp.bfloat16)


def dot_parts(a, b, contract_a, contract_b):
    a, b = tuple(a), tuple(b)
    rows = a[0].shape[0]

    def dot(x, y):
        return lax.dot_general(
            x, y, (((contract_a,), (contract_b,)), ((), ())), preferred_element_type=jnp.float32
        )

    by_high = dot(jnp.concatenate(a, axis=0), b[0])
    by_middle = dot(jnp.concatenate(a[:2], axis=0), b[1])
    small = by_high[2 * rows :] + by_middle[rows:] + dot(a[0], b[2])
    return (small + (by_high[rows : 2 * rows] + by_middle[:rows])) + by_high[:rows]


def add_gram(gram_ref, parts, first, slots=None):
    blocks = upper_blocks(parts[0].shape[0] // LANES)
    slots = range(len(blocks)) if slots is None else slots
    for a in sorted({blocks[slot][0] for slot in slots}):
        row = [slot for slot in slots if blocks[slot][0] == a]
        low, high = blocks[row[0]][1] * LANES, (blocks[row[-1]][1] + 1) * LANES
        terms = dot_parts([x[a * LANES : (a + 1) * LANES] for x in parts], [x[low:high] for x in parts], 1, 1)
        for place, slot in enumerate(row):
            block = pl.ds(slot * LANES, LANES)
            term = terms[:, place * LANES : (place + 1) * LANES]
            gram_ref[block, :] = term if first else gram_ref[block, :] + term


def finish_gram(held, across, gram_ref, load_parts, first):
    nz = held.shape[0]
    count = gram_ref.shape[0] // LANES

    def start():
        for copies in across:
            for copy in copies:
                copy.start()

    if nz != 2 or count % 2:
        add_gram(gram_ref, load_parts(), first)
        held[...] = gram_ref[...].reshape(held.shape)
        start()
        return

    def half(side):
        slots = range(side * count // 2, (side + 1) * count // 2)
        add_gram(gram_ref, load_parts(), first, slots)
        rows = gram_ref[slots[0] * LANES : (slots[-1] + 1) * LANES, :]
        held[side] = rows.reshape(held.shape[1:])

    def mine_last(side):
        def body():
            half(1 - side)
            start()
            half(side)

        return body

    mz = lax.axis_index("gz")
    for side in range(2):
        pl.when(mz == side)(mine_last(side))


def whole_gram(gram):
    count = 1
    while count * (count + 1) // 2 * LANES < gram.shape[0]:
        count += 1
    block = {}
    for slot, (a, b) in enumerate(upper_blocks(count)):
        block[a, b] = gram[slot * LANES : (slot + 1) * LANES, :]
        if a != b:
            block[b, a] = block[a, b].T
    return jnp.concatenate(
        [jnp.concatenate([block[a, b] for b in range(count)], axis=1) for a in range(count)], axis=0
    )


def last_images(gram_ref, current):
    gram = parts_of(whole_gram(gram_ref[...]))
    for turn in range(ITERS):
        images = parts_of(dot_parts(parts_of(current), gram, 1, 0))
        inverse = parts_of(inverse_lower(dot_parts(images, images, 1, 1)))
        if turn < ITERS - 1:
            current = dot_parts(inverse, images, 1, 0)
    return images, inverse


def power_steps(gram_ref, current):
    images, inverse = last_images(gram_ref, current)
    return dot_parts(inverse, images, 1, 0)


def second_power_kernel(gram_ref, start_ref, rows_ref, first_ref, first_out_ref, out_ref, core_ref):
    first_out_ref[...] = first_ref[...]
    images, inverse = last_images(gram_ref, start_ref[...])
    on_images = parts_of(dot_parts(parts_of(rows_ref[...]), images, 1, 1))
    out_ref[...] = dot_parts(inverse, images, 1, 0)
    core_ref[...] = dot_parts(on_images, inverse, 1, 1)


def species_major(block, order):
    high = block.astype(jnp.bfloat16)
    left = block - high.astype(jnp.float32)
    middle = left.astype(jnp.bfloat16)
    low = (left - middle.astype(jnp.float32)).astype(jnp.bfloat16)
    moved = [
        lax.dot_general(part, order, (((1,), (0,)), ((), ())), preferred_element_type=jnp.float32)
        for part in (high, middle, low)
    ]
    return (moved[0] + moved[1]) + moved[2]


def first_exchange(n, targets, finish, x_ref, start_load, field, fibres, split, gram, packed, load_sems, send_sems, recv_sems):
    me = lax.axis_index("gx")
    depth, rows, columns = field.shape
    span = n * LANES
    cells = span // S
    width = columns // n
    chunks = columns // span
    loads = []
    for chunk in range(chunks):
        lanes = pl.ds(chunk * span, span)
        loads.append(pltpu.make_async_copy(x_ref.at[0, :, lanes], field.at[0, :, lanes], load_sems.at[chunk]))
    for z in range(1, depth):
        loads.append(pltpu.make_async_copy(x_ref.at[z], field.at[z], load_sems.at[chunks + z - 1]))
    for load in loads + [start_load]:
        load.start()
    say_hello(targets)
    peers = far_partners(n, me)
    source = lax.broadcasted_iota(jnp.int32, (span, span), 0)
    target = lax.broadcasted_iota(jnp.int32, (span, span), 1)
    species = lax.shift_right_logical(target, cells.bit_length() - 1)
    order = jnp.where(source == (target & (cells - 1)) * S + species, 1.0, 0.0).astype(jnp.bfloat16)
    copies = {level: [] for level in range(depth)}

    def transfer(level, turn, p, lanes, sem):
        copies[level].append(send(
            packed.at[level, p, :, lanes], fibres.at[level, me, :, lanes], send_sems.at[sem, turn],
            recv_sems.at[sem, turn], {"gx": p},
        ))

    for level in range(depth):
        if level > 0:
            loads[chunks + level - 1].wait()
        for chunk in range(chunks):
            if level == 0:
                loads[chunk].wait()
            moved = species_major(field[level, :, chunk * span : (chunk + 1) * span], order)
            lanes = pl.ds(chunk * LANES, LANES)
            for p in range(n):
                packed[level, p, :, lanes] = moved[:, p * LANES : (p + 1) * LANES]
            if level == 0:
                if chunk == 0:
                    hear_hello(targets)
                for turn, p in enumerate(peers):
                    transfer(level, turn, p, lanes, chunk)
        if level > 0:
            for turn, p in enumerate(peers):
                transfer(level, turn, p, pl.ds(0, width), chunks + level - 1)
        fibres[level, me] = packed[level, me]
    for level in range(depth):
        for copy in copies[level]:
            copy.wait()
        parts = parts_of(fibres[level].reshape(n * rows, width))
        for i, part in enumerate(parts):
            split[i, level] = part
        if level < depth - 1:
            add_gram(gram, parts, level == 0)
    finish(gram, lambda: [split[i, depth - 1] for i in range(3)], depth == 1)
    start_load.wait()


def second_exchange(n, cells, finish, factor, split, last, rows_ref, gram, packed, land, send_sems, recv_sems):
    me = lax.axis_index("gy")
    depth, ranks, width = packed.shape[0], packed.shape[2], packed.shape[3]
    peers = partners(n, me)
    copies = []
    factor = parts_of(factor)
    for level in range(depth):
        field = [split[i, level] for i in range(len(factor))]
        packed[level] = dot_parts(factor, field, 1, 0).reshape(n, ranks, width)
        for turn, p in enumerate(peers):
            sem = level * (n - 1) + turn
            copies.append(
                send(packed.at[level, p], land.at[me, level], send_sems.at[sem], recv_sems.at[sem], {"gy": p})
            )
        land[me, level] = packed[level, me]
    lane_group = lax.shift_right_logical(
        lax.broadcasted_iota(jnp.int32, (ranks, LANES), 1), cells.bit_length() - 1
    )
    for level in range(depth):
        for copy in copies[level * (n - 1) : (level + 1) * (n - 1)]:
            copy.wait_recv()
        chunks = width // LANES
        for tile in range(chunks):
            for s in range(n):
                merged = None
                for g in range(n):
                    t, chunk = divmod(n * tile + g, chunks)
                    turned = land[t, level, :, chunk * LANES : (chunk + 1) * LANES]
                    if g != s:
                        turned = pltpu.roll(turned, cells * ((g - s) % n), 1)
                    merged = turned if g == 0 else jnp.where(lane_group == g, turned, merged)
                rows_ref[s, level, :, tile * LANES : (tile + 1) * LANES] = merged
        if level % 2 or level == depth - 1:
            low = level - level % 2
            whole = rows_ref[:, low : level + 1].reshape(n * (level + 1 - low) * ranks, width)
            parts = parts_of(whole.T)
            if level < depth - 1:
                add_gram(gram, parts, low == 0)
            else:
                for i, part in enumerate(parts):
                    last[i] = part
                finish(gram, lambda: [last[i] for i in range(3)], low == 0)
    for copy in copies:
        copy.wait_send()


def flat_plan(rows, nx, ny, nz):
    piece = rows // (nx * ny * nz)
    count = nx * (nz - 1) + nx * ny - 1
    return (nz, nx, ny, piece, LANES), [
        pltpu.VMEM((nz - 1, nx, ny, piece, LANES), jnp.float32),
        pltpu.VMEM((nx, ny, piece, LANES), jnp.float32),
        pltpu.VMEM((nx, ny, piece, LANES), jnp.float32),
        pltpu.VMEM((nz, nx, ny, piece, LANES), jnp.float32),
        pltpu.SemaphoreType.DMA((2, count)),
        pltpu.SemaphoreType.DMA((2, count)),
    ]


def across_copies(nx, nz, held, scratch):
    land_core, send_sems, recv_sems = scratch[0], scratch[4], scratch[5]
    mx, mz = lax.axis_index("gx"), lax.axis_index("gz")
    copies = []
    for i, px in enumerate(partners(nx, mx) + [mx]):
        copies.append([])
        for d, p in enumerate(partners(nz, mz)):
            sem = i * (nz - 1) + d
            copies[-1].append(pltpu.make_async_remote_copy(
                src_ref=held.at[p, px], dst_ref=land_core.at[d, px], send_sem=send_sems.at[0, sem],
                recv_sem=recv_sems.at[0, sem], device_id={"gz": p}, device_id_type=MESH,
            ))
    return copies


def flat_reduce(nx, ny, nz, held, across, scratch):
    land_core, half, land, total, send_sems, recv_sems = scratch
    mx, my, mz = lax.axis_index("gx"), lax.axis_index("gy"), lax.axis_index("gz")
    cores, columns, planes = partners(nz, mz), partners(nx, mx), partners(ny, my)
    groups = columns + [mx]
    base = nx * (nz - 1)

    def turns(px):
        return [(px, py) for py in planes + ([] if px is mx else [my])]

    order = [(i, px, py) for i, (px, py) in enumerate(sum((turns(px) for px in groups), []))]

    copies = {}
    for i, px in enumerate(groups):
        for copy in across[i]:
            copy.wait_recv()
        summed = held[mz, px]
        for d in range(nz - 1):
            summed = summed + land_core[d, px]
        half[px] = summed
        for slot, qx, qy in order:
            if qx is px:
                copies[slot] = send(half.at[qx, qy], land.at[mx, my], send_sems.at[0, base + slot],
                                    recv_sems.at[0, base + slot], {"gx": qx, "gy": qy})
    for copy in sum(across, []):
        copy.wait_send()
    result = half[mx, my]
    for slot, qx, qy in reversed(order):
        copies[slot].wait_recv()
        result = result + land[qx, qy]
    total[mz, mx, my] = result
    own = total.at[mz, mx, my]
    back = {}
    for slot, qx, qy in order:
        back[slot] = send(own, own, send_sems.at[1, base + slot], recv_sems.at[1, base + slot], {"gx": qx, "gy": qy})
    for slot, qx, qy in order:
        copies[slot].wait_send()
    across = []
    for i, px in reversed(list(enumerate(groups))):
        for slot, qx, qy in order:
            if qx is px:
                back[slot].wait_recv()
        block = total.at[mz, px]
        for d, p in enumerate(cores):
            across.append(send(block, block, send_sems.at[1, i * (nz - 1) + d], recv_sems.at[1, i * (nz - 1) + d], {"gz": p}))
    for slot, qx, qy in order:
        back[slot].wait_send()
    for copy in across:
        copy.wait()


def stages_kernel(axes, sizes, cells, x_ref, start_ref, factor_ref, rows_ref, gram_ref, *scratch):
    nz, ny, nx = sizes
    targets = axis_peers(axes, sizes)
    gram, field, fibres, packed, load_sems, send_first, recv_first = scratch[:7]
    packed_second, land, send_second, recv_second, start, start_sem, split, last = scratch[7:15]
    half = (len(scratch) - 15) // 2
    reduces = scratch[15 : 15 + half], scratch[15 + half :]
    start_load = pltpu.make_async_copy(start_ref, start, start_sem)

    across = [across_copies(nx, nz, reduce[0], reduce[1:]) for reduce in reduces]
    finish = [functools.partial(finish_gram, reduce[0], copies) for reduce, copies in zip(reduces, across)]

    def reduced(turn, into):
        held, total = reduces[turn][0], reduces[turn][4]
        flat_reduce(nx, ny, nz, held, across[turn], reduces[turn][1:])
        into[...] = total[...].reshape(into.shape)

    first_exchange(nx, targets, finish[0], x_ref, start_load, field, fibres, split, gram, packed, load_sems, send_first, recv_first)
    reduced(0, gram)
    factor = power_steps(gram, start[...])
    factor_ref[...] = factor
    second_exchange(ny, cells, finish[1], factor, split, last, rows_ref, gram, packed_second, land, send_second, recv_second)
    reduced(1, gram_ref)


def stages(field, start, axes, sizes, cells):
    nz, ny, nx = sizes
    depth, rows, columns = field.shape
    rank, extent = start.shape
    width = columns // nx
    ranks = rank // ny
    gram_shape = (len(upper_blocks(extent // LANES)) * LANES, LANES)
    blocked, reduce_scratch = flat_plan(gram_shape[0], nx, ny, nz)
    reduce_scratch = [pltpu.VMEM(blocked, jnp.float32)] + reduce_scratch
    first, second = width // LANES + depth - 1, depth * (ny - 1)
    return pl.pallas_call(
        functools.partial(stages_kernel, axes, sizes, cells),
        out_shape=(
            jax.ShapeDtypeStruct((rank, extent), jnp.float32),
            jax.ShapeDtypeStruct((ny, depth, ranks, width), jnp.float32),
            jax.ShapeDtypeStruct(gram_shape, jnp.float32),
        ),
        in_specs=[pl.BlockSpec(memory_space=pltpu.HBM)] * 2,
        out_specs=(VMEM, VMEM, VMEM),
        scratch_shapes=[
            pltpu.VMEM(gram_shape, jnp.float32),
            pltpu.VMEM((depth, rows, columns), jnp.float32),
            pltpu.VMEM((depth, nx, rows, width), jnp.float32),
            pltpu.VMEM((depth, nx, rows, width), jnp.float32),
            pltpu.SemaphoreType.DMA((first,)),
            pltpu.SemaphoreType.DMA((first, nx - 1)),
            pltpu.SemaphoreType.DMA((first, nx - 1)),
            pltpu.VMEM((depth, ny, ranks, width), jnp.float32),
            pltpu.VMEM((ny, depth, ranks, width), jnp.float32),
            pltpu.SemaphoreType.DMA((second,)),
            pltpu.SemaphoreType.DMA((second,)),
            pltpu.VMEM((rank, extent), jnp.float32),
            pltpu.SemaphoreType.DMA,
            pltpu.VMEM((3, depth, extent, width), jnp.bfloat16),
            pltpu.VMEM((3, width, (2 - depth % 2) * rank), jnp.bfloat16),
            *reduce_scratch,
            *reduce_scratch,
        ],
        compiler_params=pltpu.CompilerParams(collective_id=0, has_side_effects=True, vmem_limit_bytes=GRANT),
    )(field, start)


def in_hbm(x):
    return pltpu.with_memory_space_constraint(x, pltpu.HBM)


def local(nx, ny, nz, species_field, start_first, start_second):
    depth, rows, columns = species_field.shape
    rank, extent = start_first.shape[1], start_second.shape[0]
    species, ranks = S // nx, rank // ny
    cells = LANES // species
    fits = (
        columns % (nx * LANES) == 0
        and columns // nx == extent
        and nx * rows == extent
        and species == ny
        and extent % LANES == 0
        and nx * rows % LANES == 0
        and ranks % 8 == 0
        and rank % 16 == 0
        and len(upper_blocks(extent // LANES)) * LANES % (8 * nx * ny * nz) == 0
    )
    if not fits:
        return local_general(nx, ny, nz, species_field, start_first, start_second)
    axes, sizes = ("gz", "gy", "gx"), (nz, ny, nx)
    factor_first, rows_second, gram_second = stages(in_hbm(species_field), in_hbm(start_first.T), axes, sizes, cells)
    rows_second = rows_second.reshape(species * depth * ranks, extent)
    factor_first, factor_second, core = pl.pallas_call(
        second_power_kernel,
        out_shape=(
            jax.ShapeDtypeStruct((rank, extent), jnp.float32),
            jax.ShapeDtypeStruct((rank, extent), jnp.float32),
            jax.ShapeDtypeStruct((rows_second.shape[0], rank), jnp.float32),
        ),
        in_specs=[VMEM, VMEM, VMEM, VMEM],
        out_specs=(VMEM, VMEM, VMEM),
        compiler_params=pltpu.CompilerParams(vmem_limit_bytes=GRANT),
    )(gram_second, start_second.T, rows_second, factor_first)
    return (factor_first.T, factor_second.T, core.reshape(species, depth, ranks, rank))


def solution(mesh):
    return jax.shard_map(
        functools.partial(local, mesh.shape["gx"], mesh.shape["gy"], mesh.shape["gz"]),
        mesh=mesh,
        in_specs=(P("gz", "gx", "gy"), P(), P()),
        out_specs=(P(), P(), P("gx", "gz", "gy", None)),
        check_vma=False,
    )
```
